32 devices in a mesh: groups: 2 (over x), pair: 16 (over z, y, core).
Axes of the slice: x: 2, y: 2, z: 4, core: 2. Of those that a mesh axis runs over, the one named last changes fastest.
Arguments:
- chol: bfloat16 [2048, 262144], P('groups', 'pair'), parts along dimension 0, may hold values from -0.3125 to 0.3125
- walkers: bfloat16 [64, 512, 128], P(('groups', 'pair')), parts along dimension 0, may hold values from -6 to 6
- trial: bfloat16 [1024, 128], P('groups'), parts along dimension 0, may hold values from -0.5 to 0.5
- one_body: bfloat16 [1024, 512], P('groups'), parts along dimension 0, may hold values from -0.625 to 0.625
- fields: float32 [64, 1024], P(('groups', 'pair')), parts along dimension 0, may hold values from -6 to 6
- src_shift: int32 [64], P(('groups', 'pair')), parts along dimension 0, may hold values from -1 to 1
- src_slot: int32 [64], P(('groups', 'pair')), parts along dimension 0, may hold values from 0 to 1
Outputs:
- next_walkers: bfloat16 [64, 512, 128], P(('groups', 'pair')), parts along dimension 0
The draws below stay inside these ranges and needn't reach their ends.
There are 2 independent parts, one for each index of `groups`. The reference program is written for one: setup_inputs(seed, part) draws one part's arguments, and reference() takes and returns one part's arrays. A program takes and returns all parts, laid end to end along the dimension named above; each array names one. Nothing has to cross between parts.
All inputs are finite; a program needn't handle non-finite values.
Results may differ from the reference program's by a relative error of at most 0.012.
Values may be sent and summed in bfloat16 or wider, within the bound.
No kernel may reach another device: no remote copies, remote signals or barrier semaphores. Data moves between devices by JAX's collectives and lax.ppermute only.
A program may use at most 64 MiB of HBM per device.

```python
import jax
import jax.numpy as jnp
from jax import lax

N = 512
NOCC = 128
NG = 1024
TERMS = 6
W_DEV = 2
WALKERS = 32
PAIRS = 262144
N_PAIR = 16


def set_ends(values, key, low, largest):
    place = [jax.random.randint(jax.random.fold_in(key, axis), (), 0, length) for axis, length in enumerate(values.shape)]
    longest = values.shape.index(max(values.shape))
    beside = place[:longest] + [(place[longest] + 1) % values.shape[longest]] + place[longest + 1:]
    return values.at[tuple(place)].set(low).at[tuple(beside)].set(largest)


def block_levels(rng, extent, cuts, smallest, top_value):
    def one(dim, shards_of):
        steps = jax.random.uniform(jax.random.fold_in(jax.random.fold_in(rng, 6), dim), (shards_of,), jnp.float32, smallest / len(cuts), top_value / len(cuts))
        return jnp.repeat(jnp.exp(steps), extent[dim] // shards_of).reshape((-1,) + (1,) * (len(extent) - dim - 1))

    loudness = one(*cuts[0])
    for cut in cuts[1:]:
        loudness = loudness * one(*cut)
    return loudness


def centred(stream_key, shape, deviation, reach, split=(), held_as=jnp.bfloat16):
    level = block_levels(stream_key, shape, split, -0.22, 0.18) if split else 1.0
    values = jax.random.normal(stream_key, shape, jnp.float32) * deviation * level
    return jnp.minimum(jnp.maximum(values, -reach), reach).astype(held_as)


def setup_inputs(seed: int = 0, part: int = 0) -> dict:
    key_of = jax.random.split(jax.random.key(seed), 8)
    part_keys = jax.random.split(jax.random.fold_in(key_of[7], part), 8)
    return {
        "chol": centred(part_keys[0], (NG, PAIRS), (10.0 / N), 0.3125, ((1, 16),)),
        "walkers": centred(part_keys[1], (WALKERS, N, NOCC), 1.0, 6.0, ((0, 16),)),
        "trial": centred(part_keys[2], (N, NOCC), NOCC ** -0.5, 0.5),
        "one_body": centred(part_keys[3], (N, N), (0.9 / N ** 0.5), 0.625),
        "fields": centred(part_keys[4], (WALKERS, NG), 1.0, 6.0, ((0, 16),), jnp.float32),
        "src_shift": set_ends(jax.random.randint(part_keys[5], (WALKERS,), -1, 2), jax.random.fold_in(part_keys[5], 1), -1, 1).astype(jnp.int32),
        "src_slot": set_ends(jax.random.randint(part_keys[6], (WALKERS,), 0, W_DEV), jax.random.fold_in(part_keys[6], 1), 0, W_DEV - 1).astype(jnp.int32),
    }


sqrt_tau = 0.1
bias_cap = 1.0

def taylor(amat, block):
    a_full = amat.astype(jnp.float32)
    term = block
    total = block.astype(jnp.float32)
    for order in range(1, TERMS):
        product = jnp.einsum('wik,wka->wia', a_full, term.astype(jnp.float32)) / order
        total = total + product
        term = product.astype(jnp.bfloat16)
    return total.astype(jnp.bfloat16)

def reference(chol, walkers, trial, one_body, fields, src_shift, src_slot):
    chol_full = chol.astype(jnp.float32)
    trial_full = trial.astype(jnp.float32)
    blocks = walkers.reshape(N_PAIR, W_DEV, N, NOCC)

    def bias_block(block):
        green = jnp.einsum('wia,ka->wik', block.astype(jnp.float32), trial_full).astype(jnp.bfloat16)
        green = green.reshape(W_DEV, N * N).astype(jnp.float32)
        return lax.dot_general(green, chol_full, (((1,), (1,)), ((), ())))
    force = sqrt_tau * lax.map(bias_block, blocks).reshape(WALKERS, NG)
    shift = (fields - jnp.clip(force, -bias_cap, bias_cap)).astype(jnp.bfloat16)
    shift_blocks = shift.reshape(N_PAIR, W_DEV, NG)
    body_term = one_body.astype(jnp.float32)

    def propagate(pieces):
        shift_part, block = pieces
        potential = (sqrt_tau * jnp.dot(shift_part.astype(jnp.float32), chol_full)).astype(jnp.bfloat16)
        amat = (potential.astype(jnp.float32).reshape(W_DEV, N, N) + body_term).astype(jnp.bfloat16)
        return taylor(amat, block)
    propagated = lax.map(propagate, (shift_blocks, blocks)).reshape(WALKERS, N, NOCC)
    owner = jnp.arange(WALKERS, dtype=jnp.int32) // W_DEV
    source = ((owner + src_shift) % N_PAIR * W_DEV + src_slot).astype(jnp.int32)
    return jnp.take(propagated, source, axis=0)
```

```python
import jax
import jax.numpy as jnp
from jax import lax
from jax.experimental import pallas as pl
from jax.experimental.pallas import tpu as pltpu
from jax.sharding import PartitionSpec as P

TERMS = 6
LANES = 128
MIB = 1 << 20

sqrt_tau = 0.1
bias_cap = 1.0

VMEM = pl.BlockSpec(memory_space=pltpu.VMEM)
SMEM = pl.BlockSpec(memory_space=pltpu.SMEM)
ANY = pl.BlockSpec(memory_space=pl.ANY)


def params(mib):
    return pltpu.CompilerParams(vmem_limit_bytes=mib * MIB)


def in_vmem(array):
    return pltpu.with_memory_space_constraint(array, pltpu.VMEM)


def exchange(blocks):
    return lax.all_to_all(blocks, "pair", split_axis=0, concat_axis=0, tiled=True)


def neighbours(block):
    count = lax.axis_size("pair")
    forward = [(i, (i + 1) % count) for i in range(count)]
    backward = [(target, source) for source, target in forward]
    return lax.ppermute(block, "pair", forward), lax.ppermute(block, "pair", backward)


def fold_trial(chol, trial):
    vectors, pairs = chol.shape
    orbitals, occupied = trial.shape
    rows = pairs // orbitals
    per = 4

    def body(chol_ref, trial_ref, folded_ref):
        for row in range(per):
            folded_ref[:, row * occupied : (row + 1) * occupied] = jnp.dot(
                chol_ref[:, row * orbitals : (row + 1) * orbitals],
                trial_ref[...],
                preferred_element_type=jnp.float32,
            ).astype(jnp.bfloat16)

    return pl.pallas_call(
        body,
        out_shape=pltpu.HBM((vectors, rows * occupied), jnp.bfloat16),
        grid=(rows // per,),
        in_specs=[
            pl.BlockSpec((vectors, per * orbitals), lambda i: (0, i)),
            pl.BlockSpec((orbitals, occupied), lambda i: (0, 0)),
        ],
        out_specs=pl.BlockSpec((vectors, per * occupied), lambda i: (0, i)),
        compiler_params=params(24),
        cost_estimate=pl.CostEstimate(
            flops=2 * vectors * pairs * occupied, bytes_accessed=2 * vectors * pairs, transcendentals=0
        ),
        name="fold_trial",
    )(chol, trial)


def bias_partial(moved, folded):
    walkers, depth = moved.shape
    vectors = folded.shape[0]
    strips = vectors // LANES
    steps = 4
    each = strips // steps

    def body(moved_ref, folded_ref, out_ref, acc_ref):
        step = pl.program_id(0)
        part = lax.dot_general(
            moved_ref[...], folded_ref[...], (((1,), (1,)), ((), ())), preferred_element_type=jnp.float32
        )
        for strip in range(each):
            acc_ref[pl.ds(step * each + strip, walkers, stride=strips), :] = part[
                :, strip * LANES : (strip + 1) * LANES
            ]

        @pl.when(step == steps - 1)
        def _():
            out_ref[...] = acc_ref[...].astype(jnp.bfloat16)

    return pl.pallas_call(
        body,
        out_shape=jax.ShapeDtypeStruct((walkers * strips, LANES), jnp.bfloat16),
        grid=(steps,),
        in_specs=[
            pl.BlockSpec((walkers, depth), lambda i: (0, 0)),
            pl.BlockSpec((vectors // steps, depth), lambda i: (i, 0)),
        ],
        out_specs=pl.BlockSpec((walkers * strips, LANES), lambda i: (0, 0)),
        scratch_shapes=[pltpu.VMEM((walkers * strips, LANES), jnp.float32)],
        compiler_params=params(10),
        name="bias_partial",
    )(moved, pltpu.with_memory_space_constraint(folded, pltpu.HBM))


def shift_blocks(partials, fields, table):
    count, strips, _ = partials.shape

    def body(partials_ref, fields_ref, table_ref, out_ref):
        total = jnp.sum(partials_ref[...].astype(jnp.float32), axis=0)
        shift = fields_ref[...] - jnp.clip(sqrt_tau * total, -bias_cap, bias_cap)
        block = jnp.concatenate([shift, table_ref[...]], axis=0).astype(jnp.bfloat16)
        out_ref[...] = jnp.broadcast_to(block[None], out_ref.shape)

    return pl.pallas_call(
        body,
        out_shape=jax.ShapeDtypeStruct((count, strips + table.shape[0], LANES), jnp.bfloat16),
        in_specs=[VMEM, VMEM, VMEM],
        out_specs=VMEM,
        compiler_params=params(4),
        name="shift_blocks",
    )(partials, fields, table)


def potential(blocks, chol, w_local, orbitals):
    count, height, _ = blocks.shape
    vectors, pairs = chol.shape
    rows = pairs // orbitals
    each = vectors // LANES
    walkers = count * w_local
    group = 8

    def body(blocks_ref, chol_ref, out_ref, wide_ref, shift_ref, acc_ref):
        wide_ref[...] = blocks_ref[...].astype(jnp.float32).reshape(count * height, LANES)
        for slot in range(w_local):
            for strip in range(each):
                shift_ref[pl.ds(slot * count, count), pl.ds(strip * LANES, LANES)] = wide_ref[
                    pl.ds(slot * each + strip, count, stride=height), :
                ].astype(jnp.bfloat16)
        table = wide_ref[pl.ds(w_local * each, count, stride=height), :]
        device = lax.broadcasted_iota(jnp.int32, (count, walkers), 0).astype(jnp.float32)
        place = lax.broadcasted_iota(jnp.int32, (count, walkers), 1).astype(jnp.float32)
        picks = []
        for slot in range(w_local):
            parent = device + table[:, slot : slot + 1]
            parent = jnp.where(parent < 0, parent + count, parent)
            parent = jnp.where(parent >= count, parent - count, parent)
            parent = parent + count * table[:, w_local + slot : w_local + slot + 1]
            picks.append(jnp.where(place == parent, 1.0, 0.0))
        pick = jnp.concatenate(picks, axis=0).astype(jnp.bfloat16)
        shift = jnp.dot(pick, shift_ref[...], preferred_element_type=jnp.float32).astype(jnp.bfloat16)

        @pl.loop(0, rows // group)
        def _(step):
            for inner in range(group):
                row = step * group + inner
                cols = pl.ds(pl.multiple_of(row * orbitals, orbitals), orbitals)
                part = sqrt_tau * jnp.dot(shift, chol_ref[:, cols], preferred_element_type=jnp.float32)
                for slot in range(w_local):
                    for lane in range(orbitals // LANES):
                        acc_ref[lane, pl.ds(slot * group + inner, count, stride=w_local * group), :] = part[
                            slot * count : (slot + 1) * count, lane * LANES : (lane + 1) * LANES
                        ]
            for lane in range(orbitals // LANES):
                done = acc_ref[lane].reshape(count, w_local, group, LANES).astype(jnp.bfloat16)
                for slot in range(w_local):
                    start = pl.multiple_of(slot * rows + step * group, group)
                    out_ref[:, pl.ds(start, group), pl.ds(lane * LANES, LANES)] = done[:, slot]

    return pl.pallas_call(
        body,
        out_shape=jax.ShapeDtypeStruct((count, w_local * rows, orbitals), jnp.bfloat16),
        in_specs=[VMEM, VMEM],
        out_specs=VMEM,
        scratch_shapes=[
            pltpu.VMEM((count * height, LANES), jnp.float32),
            pltpu.VMEM((walkers, vectors), jnp.bfloat16),
            pltpu.VMEM((orbitals // LANES, walkers * group, LANES), jnp.float32),
        ],
        compiler_params=params(10),
        name="potential",
    )(blocks, chol)


def propagate(blocks, one_body, low, own, high, src_shift, src_slot):
    w_local, orbitals, occupied = own.shape
    count, height, _ = blocks.shape
    rows = height // w_local

    def body(blocks_ref, one_ref, low_ref, own_ref, high_ref, shift_ref, slot_ref, out_ref, start_ref):
        one = one_ref[...].astype(jnp.float32)
        for walker in range(w_local):
            for offset, source in ((-1, low_ref), (0, own_ref), (1, high_ref)):

                @pl.when(shift_ref[walker] == offset)
                def _():
                    start_ref[...] = source[slot_ref[walker]]

            mine = blocks_ref[:, walker * rows : (walker + 1) * rows, :]
            amat = mine.astype(jnp.float32).reshape(orbitals, orbitals) + one
            amat = amat.astype(jnp.bfloat16)
            term = start_ref[...]
            total = term.astype(jnp.float32)
            for order in range(1, TERMS):
                product = jnp.dot(amat, term, preferred_element_type=jnp.float32) / order
                total = total + product
                term = product.astype(jnp.bfloat16)
            out_ref[walker] = total.astype(jnp.bfloat16)

    return pl.pallas_call(
        body,
        out_shape=jax.ShapeDtypeStruct(own.shape, jnp.bfloat16),
        in_specs=[VMEM, VMEM, VMEM, VMEM, VMEM, SMEM, SMEM],
        out_specs=VMEM,
        scratch_shapes=[pltpu.VMEM((orbitals, occupied), jnp.bfloat16)],
        compiler_params=params(16),
        name="propagate",
    )(blocks, one_body, low, own, high, src_shift, src_slot)


def plain(chol, walkers, trial, one_body, fields, src_shift, src_slot):
    count = lax.axis_size("pair")
    w_local, orbitals, _ = walkers.shape
    moved = lax.all_to_all(walkers, "pair", split_axis=1, concat_axis=0, tiled=True)
    formed = jnp.einsum("wia,ka->wik", moved, trial, preferred_element_type=jnp.float32)
    green_rows = formed.astype(jnp.bfloat16).reshape(moved.shape[0], moved.shape[1] * orbitals)
    partial_bias = lax.dot_general(
        green_rows, chol, (((1,), (1,)), ((), ())), preferred_element_type=jnp.float32
    )
    partials = exchange(partial_bias).reshape(count, w_local, -1)
    total = jnp.sum(partials, axis=0)
    shift = (fields - jnp.clip(sqrt_tau * total, -bias_cap, bias_cap)).astype(jnp.bfloat16)
    shifts = exchange(jnp.broadcast_to(shift[None], (count,) + shift.shape))
    shifts = shifts.reshape(count * w_local, -1)
    local_potential = (sqrt_tau * jnp.dot(shifts, chol, preferred_element_type=jnp.float32)).astype(
        jnp.bfloat16
    )
    own_potential = lax.all_to_all(local_potential, "pair", split_axis=0, concat_axis=1, tiled=True)
    amat = own_potential.astype(jnp.float32).reshape(w_local, orbitals, orbitals) + one_body.astype(
        jnp.float32
    )
    amat = amat.astype(jnp.bfloat16)
    term = walkers
    total = walkers.astype(jnp.float32)
    for order in range(1, TERMS):
        product = jnp.einsum("wik,wka->wia", amat, term, preferred_element_type=jnp.float32) / order
        total = total + product
        term = product.astype(jnp.bfloat16)
    propagated = total.astype(jnp.bfloat16)
    low, high = neighbours(propagated)
    position = (src_shift + 1) * w_local + src_slot
    return jnp.take(jnp.concatenate([low, propagated, high], axis=0), position, axis=0)


def held(chol, walkers, trial, one_body, fields, src_shift, src_slot):
    count = lax.axis_size("pair")
    w_local, orbitals, occupied = walkers.shape
    vectors, pairs = chol.shape
    rows = pairs // orbitals
    strips = w_local * vectors // LANES

    low, high = neighbours(walkers)
    sent = walkers.reshape(w_local, count, rows, occupied).transpose(1, 0, 2, 3)
    moved = exchange(sent.reshape(count, w_local * rows, occupied))
    folded = fold_trial(chol, trial)
    moved = moved.reshape(count * w_local, rows * occupied)
    entries = jnp.concatenate([src_shift, src_slot]).astype(jnp.float32)
    table = jnp.zeros((8, LANES), jnp.float32).at[0, : 2 * w_local].set(entries)
    fields = fields.reshape(strips, LANES)
    moved, table, fields = lax.optimization_barrier((moved, table, fields))
    partial = bias_partial(moved, folded).reshape(count, strips, LANES)
    partials = exchange(partial)
    blocks = exchange(shift_blocks(partials, fields, table))
    received = exchange(potential(blocks, chol, w_local, orbitals))
    return propagate(received, one_body, low, walkers, high, src_shift, src_slot)


def shards(chol, walkers, *rest):
    rows = chol.shape[1] // walkers.shape[1]
    fits = 2 * chol.size <= 32 * MIB and rows % 16 == 0 and chol.shape[0] % LANES == 0
    return (held if fits else plain)(chol, walkers, *rest)


def solution(mesh):
    placed = (
        P("groups", "pair"),
        P(("groups", "pair"), None, None),
        P("groups", None),
        P("groups", None),
        P(("groups", "pair"), None),
        P(("groups", "pair")),
        P(("groups", "pair")),
    )
    return jax.shard_map(
        shards,
        mesh=mesh,
        in_specs=placed,
        out_specs=P(("groups", "pair"), None, None),
        check_vma=False,
    )
```

```python
import jax
import jax.numpy as jnp
from jax import lax
from jax.experimental import pallas as pl
from jax.experimental.pallas import tpu as pltpu
from jax.sharding import PartitionSpec as P


TERMS = 6
LANES = 128
MIB = 1 << 20
GROUP = 8
COVER = pl.CostEstimate(flops=100_000_000_000, bytes_accessed=400_000_000, transcendentals=0)

sqrt_tau = 0.1
bias_cap = 1.0

VMEM = pl.BlockSpec(memory_space=pltpu.VMEM)
SMEM = pl.BlockSpec(memory_space=pltpu.SMEM)
ANY = pl.BlockSpec(memory_space=pl.ANY)


def params(mib):
    return pltpu.CompilerParams(vmem_limit_bytes=mib * MIB)


def exchange(blocks):
    return lax.all_to_all(blocks, "pair", split_axis=0, concat_axis=0, tiled=True)


def neighbours(block):
    count = lax.axis_size("pair")
    forward = [(i, (i + 1) % count) for i in range(count)]
    backward = [(target, source) for source, target in forward]
    return lax.ppermute(block, "pair", forward), lax.ppermute(block, "pair", backward)


def pack(walkers, count):
    w_local, orbitals, occupied = walkers.shape
    rows = orbitals // count

    def body(in_ref, out_ref):
        for walker in range(w_local):
            out_ref[:, walker * rows : (walker + 1) * rows, :] = in_ref[walker].reshape(count, rows, occupied)

    return pl.pallas_call(
        body,
        out_shape=jax.ShapeDtypeStruct((count, w_local * rows, occupied), jnp.bfloat16),
        in_specs=[VMEM],
        out_specs=VMEM,
        compiler_params=params(4),
        cost_estimate=COVER,
        name="pack",
    )(walkers)


def bias_partial(moved, trial, chol, w_local):
    count, height, occupied = moved.shape
    orbitals = trial.shape[0]
    vectors, pairs = chol.shape
    rows = pairs // orbitals
    walkers = count * w_local
    strips = vectors // LANES
    steps = 4
    width = pairs // steps

    def body(moved_ref, trial_ref, chol_ref, out_ref, wide_ref, lhs_ref, green_ref, acc_ref, flat_ref):
        wide_ref[...] = moved_ref[...].astype(jnp.float32).reshape(count * height, occupied)
        for row in range(rows):
            lhs_ref[row * walkers : (row + 1) * walkers, :] = wide_ref[
                pl.ds(row, walkers, stride=rows), :
            ].astype(jnp.bfloat16)
        formed = lax.dot_general(
            lhs_ref[...], trial_ref[...], (((1,), (1,)), ((), ())), preferred_element_type=jnp.float32
        )
        for row in range(rows):
            green_ref[:, row * orbitals : (row + 1) * orbitals] = formed[
                row * walkers : (row + 1) * walkers, :
            ].astype(jnp.bfloat16)
        acc_ref[...] = jnp.zeros_like(acc_ref)

        @pl.loop(0, steps)
        def _(step):
            cols = pl.ds(pl.multiple_of(step * width, width), width)
            acc_ref[...] += lax.dot_general(
                chol_ref[:, cols], green_ref[:, cols], (((1,), (1,)), ((), ())), preferred_element_type=jnp.float32
            )

        for strip in range(strips):
            flat_ref[pl.ds(strip, walkers, stride=strips), :] = acc_ref[strip * LANES : (strip + 1) * LANES, :].T
        out_ref[...] = flat_ref[...].astype(jnp.bfloat16).reshape(out_ref.shape)

    return pl.pallas_call(
        body,
        out_shape=jax.ShapeDtypeStruct((count, w_local * strips, LANES), jnp.bfloat16),
        in_specs=[VMEM, VMEM, VMEM],
        out_specs=VMEM,
        scratch_shapes=[
            pltpu.VMEM((count * height, occupied), jnp.float32),
            pltpu.VMEM((count * height, occupied), jnp.bfloat16),
            pltpu.VMEM((walkers, pairs), jnp.bfloat16),
            pltpu.VMEM((vectors, walkers), jnp.float32),
            pltpu.VMEM((walkers * strips, LANES), jnp.float32),
        ],
        compiler_params=params(16),
        name="bias_partial",
    )(moved, trial, chol)


def shift_blocks(partials, fields, src_shift, src_slot):
    count, strips, _ = partials.shape
    w_local, vectors = fields.shape
    each = vectors // LANES

    def body(partials_ref, fields_ref, from_ref, slot_ref, out_ref, flat_ref):
        for walker in range(w_local):
            for strip in range(each):
                flat_ref[walker * each + strip, :] = fields_ref[walker, strip * LANES : (strip + 1) * LANES]
        total = jnp.sum(partials_ref[...].astype(jnp.float32), axis=0)
        shift = flat_ref[...] - jnp.clip(sqrt_tau * total, -bias_cap, bias_cap)
        lane = lax.broadcasted_iota(jnp.int32, (8, LANES), 1)
        table = jnp.zeros((8, LANES), jnp.int32)
        for walker in range(w_local):
            table = jnp.where(lane == walker, from_ref[walker], table)
            table = jnp.where(lane == w_local + walker, slot_ref[walker], table)
        block = jnp.concatenate([shift, table.astype(jnp.float32)], axis=0).astype(jnp.bfloat16)
        out_ref[...] = jnp.broadcast_to(block[None], out_ref.shape)

    return pl.pallas_call(
        body,
        out_shape=jax.ShapeDtypeStruct((count, strips + 8, LANES), jnp.bfloat16),
        in_specs=[VMEM, VMEM, SMEM, SMEM],
        out_specs=VMEM,
        scratch_shapes=[pltpu.VMEM((strips, LANES), jnp.float32)],
        compiler_params=params(4),
        cost_estimate=COVER,
        name="shift_blocks",
    )(partials, fields, src_shift, src_slot)


def parents_shift(blocks_ref, wide_ref, shift_ref, w_local, each):
    count, height, _ = blocks_ref.shape
    walkers = count * w_local
    wide_ref[...] = blocks_ref[...].astype(jnp.float32).reshape(count * height, LANES)
    for slot in range(w_local):
        for strip in range(each):
            shift_ref[slot * count : (slot + 1) * count, strip * LANES : (strip + 1) * LANES] = wide_ref[
                pl.ds(slot * each + strip, count, stride=height), :
            ].astype(jnp.bfloat16)
    table = wide_ref[pl.ds(w_local * each, count, stride=height), :]
    device = lax.broadcasted_iota(jnp.int32, (count, walkers), 0).astype(jnp.float32)
    place = lax.broadcasted_iota(jnp.int32, (count, walkers), 1).astype(jnp.float32)
    picks = []
    for slot in range(w_local):
        parent = device + table[:, slot : slot + 1]
        parent = jnp.where(parent < 0, parent + count, parent)
        parent = jnp.where(parent >= count, parent - count, parent)
        parent = parent + count * table[:, w_local + slot : w_local + slot + 1]
        picks.append(jnp.where(place == parent, 1.0, 0.0))
    pick = jnp.concatenate(picks, axis=0).astype(jnp.bfloat16)
    return jnp.dot(pick, shift_ref[...], preferred_element_type=jnp.float32).astype(jnp.bfloat16)


def spread(part, acc_ref, inner, count, w_local, group):
    for slot in range(w_local):
        for lane in range(part.shape[1] // LANES):
            acc_ref[lane, pl.ds(slot * group + inner, count, stride=w_local * group), :] = part[
                slot * count : (slot + 1) * count, lane * LANES : (lane + 1) * LANES
            ]


def settle(acc_ref, out_ref, start, count, w_local, group, rows):
    for lane in range(acc_ref.shape[0]):
        done = acc_ref[lane].reshape(count, w_local, group, LANES).astype(jnp.bfloat16)
        for slot in range(w_local):
            out_ref[:, pl.ds(pl.multiple_of(slot * rows + start, group), group), pl.ds(lane * LANES, LANES)] = done[
                :, slot
            ]


def potential_held(blocks, chol, w_local, orbitals, rows):
    count, height, _ = blocks.shape
    vectors = chol.shape[0]
    walkers = count * w_local
    each = vectors // LANES

    def body(blocks_ref, chol_ref, out_ref, picked_ref, wide_ref, shift_ref, acc_ref):
        shift = parents_shift(blocks_ref, wide_ref, shift_ref, w_local, each)
        picked_ref[...] = shift

        @pl.loop(0, rows // GROUP)
        def _(step):
            for pair in range(0, GROUP, 4):
                start = (step * GROUP + pair) * orbitals
                cols = pl.ds(pl.multiple_of(start, 4 * orbitals), 4 * orbitals)
                part = sqrt_tau * jnp.dot(shift, chol_ref[:, cols], preferred_element_type=jnp.float32)
                for inner in range(4):
                    spread(
                        part[:, inner * orbitals : (inner + 1) * orbitals], acc_ref, pair + inner, count, w_local, GROUP
                    )
            settle(acc_ref, out_ref, step * GROUP, count, w_local, GROUP, rows)

    return pl.pallas_call(
        body,
        out_shape=(
            jax.ShapeDtypeStruct((count, w_local * rows, orbitals), jnp.bfloat16),
            jax.ShapeDtypeStruct((walkers, vectors), jnp.bfloat16),
        ),
        in_specs=[VMEM, VMEM],
        out_specs=(VMEM, VMEM),
        scratch_shapes=[
            pltpu.VMEM((count * height, LANES), jnp.float32),
            pltpu.VMEM((walkers, vectors), jnp.bfloat16),
            pltpu.VMEM((orbitals // LANES, walkers * GROUP, LANES), jnp.float32),
        ],
        compiler_params=params(12),
        name="potential_held",
    )(blocks, chol)


def potential_streamed(shift, chol, w_local, orbitals, first, rows):
    walkers, vectors = shift.shape
    count = walkers // w_local
    per = 4

    def body(shift_ref, chol_ref, out_ref, acc_ref):
        step = pl.program_id(0)
        half = lax.rem(step, GROUP // per)
        part = sqrt_tau * jnp.dot(shift_ref[...], chol_ref[...], preferred_element_type=jnp.float32)
        for inner in range(per):
            spread(
                part[:, inner * orbitals : (inner + 1) * orbitals], acc_ref, half * per + inner, count, w_local, GROUP
            )

        @pl.when(half == GROUP // per - 1)
        def _():
            settle(acc_ref, out_ref, (step * per) // GROUP * GROUP, count, w_local, GROUP, rows)

    return pl.pallas_call(
        body,
        out_shape=jax.ShapeDtypeStruct((count, w_local * rows, orbitals), jnp.bfloat16),
        grid=(rows // per,),
        in_specs=[
            pl.BlockSpec((walkers, vectors), lambda i: (0, 0)),
            pl.BlockSpec((vectors, per * orbitals), lambda i: (0, first // per + i)),
        ],
        out_specs=pl.BlockSpec((count, w_local * rows, orbitals), lambda i: (0, 0, 0)),
        scratch_shapes=[pltpu.VMEM((orbitals // LANES, walkers * GROUP, LANES), jnp.float32)],
        compiler_params=params(20),
        cost_estimate=pl.CostEstimate(
            flops=2 * walkers * vectors * rows * orbitals, bytes_accessed=2 * vectors * rows * orbitals, transcendentals=0
        ),
        name="potential_streamed",
    )(shift, pltpu.with_memory_space_constraint(chol, pltpu.HBM))


def propagate(early, late, one_body, low, own, high, src_shift, src_slot):
    w_local, orbitals, occupied = own.shape
    count = early.shape[0]
    rows = orbitals // count
    cut = early.shape[1] // w_local

    def body(early_ref, late_ref, one_ref, low_ref, own_ref, high_ref, from_ref, slot_ref, out_ref, start_ref, mat_ref):
        one = one_ref[...].astype(jnp.float32).reshape(count, rows, orbitals)
        for walker in range(w_local):
            for offset, source in ((-1, low_ref), (0, own_ref), (1, high_ref)):

                @pl.when(from_ref[walker] == offset)
                def _():
                    start_ref[...] = source[slot_ref[walker]]

            for ref, low_row, high_row in ((early_ref, 0, cut), (late_ref, cut, rows)):
                tall = high_row - low_row
                mine = ref[:, walker * tall : (walker + 1) * tall, :].astype(jnp.float32)
                mat_ref[:, low_row:high_row, :] = (mine + one[:, low_row:high_row, :]).astype(jnp.bfloat16)
            amat = mat_ref[...].reshape(orbitals, orbitals)
            term = start_ref[...]
            total = term.astype(jnp.float32)
            for order in range(1, TERMS):
                product = jnp.dot(amat, term, preferred_element_type=jnp.float32) / order
                total = total + product
                term = product.astype(jnp.bfloat16)
            out_ref[walker] = total.astype(jnp.bfloat16)

    return pl.pallas_call(
        body,
        out_shape=jax.ShapeDtypeStruct(own.shape, jnp.bfloat16),
        in_specs=[VMEM, VMEM, VMEM, VMEM, VMEM, VMEM, SMEM, SMEM],
        out_specs=VMEM,
        scratch_shapes=[
            pltpu.VMEM((orbitals, occupied), jnp.bfloat16),
            pltpu.VMEM((count, rows, orbitals), jnp.bfloat16),
        ],
        compiler_params=params(16),
        name="propagate",
    )(early, late, one_body, low, own, high, src_shift, src_slot)


def plain(chol, walkers, trial, one_body, fields, src_shift, src_slot):
    count = lax.axis_size("pair")
    w_local, orbitals, _ = walkers.shape
    moved = lax.all_to_all(walkers, "pair", split_axis=1, concat_axis=0, tiled=True)
    formed = jnp.einsum("wia,ka->wik", moved, trial, preferred_element_type=jnp.float32)
    green_rows = formed.astype(jnp.bfloat16).reshape(moved.shape[0], moved.shape[1] * orbitals)
    partial_bias = lax.dot_general(
        green_rows, chol, (((1,), (1,)), ((), ())), preferred_element_type=jnp.float32
    )
    partials = exchange(partial_bias).reshape(count, w_local, -1)
    total = jnp.sum(partials, axis=0)
    shift = (fields - jnp.clip(sqrt_tau * total, -bias_cap, bias_cap)).astype(jnp.bfloat16)
    shifts = exchange(jnp.broadcast_to(shift[None], (count,) + shift.shape))
    shifts = shifts.reshape(count * w_local, -1)
    local_potential = (sqrt_tau * jnp.dot(shifts, chol, preferred_element_type=jnp.float32)).astype(
        jnp.bfloat16
    )
    own_potential = lax.all_to_all(local_potential, "pair", split_axis=0, concat_axis=1, tiled=True)
    amat = own_potential.astype(jnp.float32).reshape(w_local, orbitals, orbitals) + one_body.astype(
        jnp.float32
    )
    amat = amat.astype(jnp.bfloat16)
    term = walkers
    total = walkers.astype(jnp.float32)
    for order in range(1, TERMS):
        product = jnp.einsum("wik,wka->wia", amat, term, preferred_element_type=jnp.float32) / order
        total = total + product
        term = product.astype(jnp.bfloat16)
    propagated = total.astype(jnp.bfloat16)
    low, high = neighbours(propagated)
    position = (src_shift + 1) * w_local + src_slot
    return jnp.take(jnp.concatenate([low, propagated, high], axis=0), position, axis=0)


def held(chol, walkers, trial, one_body, fields, src_shift, src_slot):
    count = lax.axis_size("pair")
    w_local, orbitals, _ = walkers.shape
    rows = chol.shape[1] // orbitals
    cut = rows // 2

    low, high = neighbours(walkers)
    moved = exchange(pack(walkers, count))
    partials = exchange(bias_partial(moved, trial, chol, w_local))
    blocks = exchange(shift_blocks(partials, fields, src_shift, src_slot))
    early, shift = potential_held(blocks, chol, w_local, orbitals, cut)
    early = exchange(early)
    late = potential_streamed(shift, chol, w_local, orbitals, cut, rows - cut)
    late = exchange(late)
    return propagate(early, late, one_body, low, walkers, high, src_shift, src_slot)


def shards(chol, walkers, *rest):
    rows = chol.shape[1] // walkers.shape[1]
    fits = 2 * chol.size <= 32 * MIB and rows % 16 == 0 and chol.shape[0] % LANES == 0
    return (held if fits else plain)(chol, walkers, *rest)


def solution(mesh):
    placed = (
        P("groups", "pair"),
        P(("groups", "pair"), None, None),
        P("groups", None),
        P("groups", None),
        P(("groups", "pair"), None),
        P(("groups", "pair")),
        P(("groups", "pair")),
    )
    return jax.shard_map(
        shards,
        mesh=mesh,
        in_specs=placed,
        out_specs=P(("groups", "pair"), None, None),
        check_vma=False,
    )
```

```python
import jax
import jax.numpy as jnp
from jax import lax
from jax.experimental import pallas as pl
from jax.experimental.pallas import tpu as pltpu
from jax.sharding import PartitionSpec as P


TERMS = 6
LANES = 128
MIB = 1 << 20
GROUP = 8
COVER = pl.CostEstimate(flops=100_000_000_000, bytes_accessed=400_000_000, transcendentals=0)

sqrt_tau = 0.1
bias_cap = 1.0

VMEM = pl.BlockSpec(memory_space=pltpu.VMEM)
SMEM = pl.BlockSpec(memory_space=pltpu.SMEM)
ANY = pl.BlockSpec(memory_space=pl.ANY)


def params(mib):
    return pltpu.CompilerParams(vmem_limit_bytes=mib * MIB)


def exchange(blocks):
    return lax.all_to_all(blocks, "pair", split_axis=0, concat_axis=0, tiled=True)


def neighbours(block):
    count = lax.axis_size("pair")
    forward = [(i, (i + 1) % count) for i in range(count)]
    backward = [(target, source) for source, target in forward]
    return lax.ppermute(block, "pair", forward), lax.ppermute(block, "pair", backward)


def pack(walkers, count):
    w_local, orbitals, occupied = walkers.shape
    rows = orbitals // count

    def body(in_ref, out_ref):
        for walker in range(w_local):
            out_ref[:, walker * rows : (walker + 1) * rows, :] = in_ref[walker].reshape(count, rows, occupied)

    return pl.pallas_call(
        body,
        out_shape=jax.ShapeDtypeStruct((count, w_local * rows, occupied), jnp.bfloat16),
        in_specs=[VMEM],
        out_specs=VMEM,
        compiler_params=params(4),
        cost_estimate=COVER,
        name="pack",
    )(walkers)


def bias_partial(moved, trial, chol, w_local):
    count, height, occupied = moved.shape
    orbitals = trial.shape[0]
    vectors, pairs = chol.shape
    rows = pairs // orbitals
    walkers = count * w_local
    strips = vectors // LANES
    steps = 4
    width = pairs // steps

    def body(moved_ref, trial_ref, chol_ref, out_ref, wide_ref, lhs_ref, green_ref, acc_ref, flat_ref):
        wide_ref[...] = moved_ref[...].astype(jnp.float32).reshape(count * height, occupied)
        for row in range(rows):
            lhs_ref[row * walkers : (row + 1) * walkers, :] = wide_ref[
                pl.ds(row, walkers, stride=rows), :
            ].astype(jnp.bfloat16)
        formed = lax.dot_general(
            lhs_ref[...], trial_ref[...], (((1,), (1,)), ((), ())), preferred_element_type=jnp.float32
        )
        for row in range(rows):
            green_ref[:, row * orbitals : (row + 1) * orbitals] = formed[
                row * walkers : (row + 1) * walkers, :
            ].astype(jnp.bfloat16)
        acc_ref[...] = jnp.zeros_like(acc_ref)

        @pl.loop(0, steps)
        def _(step):
            cols = pl.ds(pl.multiple_of(step * width, width), width)
            acc_ref[...] += lax.dot_general(
                chol_ref[:, cols], green_ref[:, cols], (((1,), (1,)), ((), ())), preferred_element_type=jnp.float32
            )

        for strip in range(strips):
            flat_ref[pl.ds(strip, walkers, stride=strips), :] = acc_ref[strip * LANES : (strip + 1) * LANES, :].T
        out_ref[...] = flat_ref[...].astype(jnp.bfloat16).reshape(out_ref.shape)

    return pl.pallas_call(
        body,
        out_shape=jax.ShapeDtypeStruct((count, w_local * strips, LANES), jnp.bfloat16),
        in_specs=[VMEM, VMEM, VMEM],
        out_specs=VMEM,
        scratch_shapes=[
            pltpu.VMEM((count * height, occupied), jnp.float32),
            pltpu.VMEM((count * height, occupied), jnp.bfloat16),
            pltpu.VMEM((walkers, pairs), jnp.bfloat16),
            pltpu.VMEM((vectors, walkers), jnp.float32),
            pltpu.VMEM((walkers * strips, LANES), jnp.float32),
        ],
        compiler_params=params(16),
        name="bias_partial",
    )(moved, trial, chol)


def shift_blocks(partials, fields, src_shift, src_slot):
    count, strips, _ = partials.shape
    w_local, vectors = fields.shape
    each = vectors // LANES

    def body(partials_ref, fields_ref, from_ref, slot_ref, out_ref, flat_ref):
        for walker in range(w_local):
            for strip in range(each):
                flat_ref[walker * each + strip, :] = fields_ref[walker, strip * LANES : (strip + 1) * LANES]
        total = jnp.sum(partials_ref[...].astype(jnp.float32), axis=0)
        shift = flat_ref[...] - jnp.clip(sqrt_tau * total, -bias_cap, bias_cap)
        lane = lax.broadcasted_iota(jnp.int32, (8, LANES), 1)
        table = jnp.zeros((8, LANES), jnp.int32)
        for walker in range(w_local):
            table = jnp.where(lane == walker, from_ref[walker], table)
            table = jnp.where(lane == w_local + walker, slot_ref[walker], table)
        block = jnp.concatenate([shift, table.astype(jnp.float32)], axis=0).astype(jnp.bfloat16)
        out_ref[...] = jnp.broadcast_to(block[None], out_ref.shape)

    return pl.pallas_call(
        body,
        out_shape=jax.ShapeDtypeStruct((count, strips + 8, LANES), jnp.bfloat16),
        in_specs=[VMEM, VMEM, SMEM, SMEM],
        out_specs=VMEM,
        scratch_shapes=[pltpu.VMEM((strips, LANES), jnp.float32)],
        compiler_params=params(4),
        cost_estimate=COVER,
        name="shift_blocks",
    )(partials, fields, src_shift, src_slot)


def parents_shift(blocks_ref, wide_ref, shift_ref, w_local, each):
    count, height, _ = blocks_ref.shape
    walkers = count * w_local
    wide_ref[...] = blocks_ref[...].astype(jnp.float32).reshape(count * height, LANES)
    for slot in range(w_local):
        for strip in range(each):
            shift_ref[slot * count : (slot + 1) * count, strip * LANES : (strip + 1) * LANES] = wide_ref[
                pl.ds(slot * each + strip, count, stride=height), :
            ].astype(jnp.bfloat16)
    table = wide_ref[pl.ds(w_local * each, count, stride=height), :]
    device = lax.broadcasted_iota(jnp.int32, (count, walkers), 0).astype(jnp.float32)
    place = lax.broadcasted_iota(jnp.int32, (count, walkers), 1).astype(jnp.float32)
    picks = []
    for slot in range(w_local):
        parent = device + table[:, slot : slot + 1]
        parent = jnp.where(parent < 0, parent + count, parent)
        parent = jnp.where(parent >= count, parent - count, parent)
        parent = parent + count * table[:, w_local + slot : w_local + slot + 1]
        picks.append(jnp.where(place == parent, 1.0, 0.0))
    pick = jnp.concatenate(picks, axis=0).astype(jnp.bfloat16)
    return jnp.dot(pick, shift_ref[...], preferred_element_type=jnp.float32).astype(jnp.bfloat16)


def spread(part, acc_ref, inner, count, w_local, group):
    for slot in range(w_local):
        for lane in range(part.shape[1] // LANES):
            acc_ref[lane, pl.ds(slot * group + inner, count, stride=w_local * group), :] = part[
                slot * count : (slot + 1) * count, lane * LANES : (lane + 1) * LANES
            ]


def settle(acc_ref, out_ref, start, count, w_local, group, rows):
    for lane in range(acc_ref.shape[0]):
        done = acc_ref[lane].reshape(count, w_local, group, LANES).astype(jnp.bfloat16)
        for slot in range(w_local):
            out_ref[:, pl.ds(pl.multiple_of(slot * rows + start, group), group), pl.ds(lane * LANES, LANES)] = done[
                :, slot
            ]


def potential(blocks, chol, w_local, orbitals):
    count, height, _ = blocks.shape
    vectors, pairs = chol.shape
    rows = pairs // orbitals
    walkers = count * w_local
    each = vectors // LANES

    def body(blocks_ref, chol_ref, out_ref, wide_ref, shift_ref, acc_ref):
        shift = parents_shift(blocks_ref, wide_ref, shift_ref, w_local, each)

        @pl.loop(0, rows // GROUP)
        def _(step):
            for pair in range(0, GROUP, 4):
                start = (step * GROUP + pair) * orbitals
                cols = pl.ds(pl.multiple_of(start, 4 * orbitals), 4 * orbitals)
                part = sqrt_tau * jnp.dot(shift, chol_ref[:, cols], preferred_element_type=jnp.float32)
                for inner in range(4):
                    spread(
                        part[:, inner * orbitals : (inner + 1) * orbitals], acc_ref, pair + inner, count, w_local, GROUP
                    )
            settle(acc_ref, out_ref, step * GROUP, count, w_local, GROUP, rows)

    return pl.pallas_call(
        body,
        out_shape=jax.ShapeDtypeStruct((count, w_local * rows, orbitals), jnp.bfloat16),
        in_specs=[VMEM, VMEM],
        out_specs=VMEM,
        scratch_shapes=[
            pltpu.VMEM((count * height, LANES), jnp.float32),
            pltpu.VMEM((walkers, vectors), jnp.bfloat16),
            pltpu.VMEM((orbitals // LANES, walkers * GROUP, LANES), jnp.float32),
        ],
        compiler_params=params(12),
        name="potential",
    )(blocks, chol)


def propagate(blocks, one_body, low, own, high, src_shift, src_slot):
    w_local, orbitals, _ = own.shape
    count = blocks.shape[0]
    rows = orbitals // count

    def body(blocks_ref, one_ref, low_ref, own_ref, high_ref, from_ref, slot_ref, out_ref, term_ref, mat_ref):
        for walker in range(w_local):
            for offset, source in ((-1, low_ref), (0, own_ref), (1, high_ref)):

                @pl.when(from_ref[walker] == offset)
                def _():
                    term_ref[walker] = source[slot_ref[walker]]

        one = one_ref[...].astype(jnp.float32).reshape(count, rows, orbitals)
        for walker in range(w_local):
            mine = blocks_ref[:, walker * rows : (walker + 1) * rows, :].astype(jnp.float32)
            mat_ref[walker] = (mine + one).reshape(orbitals, orbitals).astype(jnp.bfloat16)
        terms = [term_ref[walker] for walker in range(w_local)]
        totals = [term.astype(jnp.float32) for term in terms]
        for order in range(1, TERMS):
            products = [
                jnp.dot(mat_ref[walker], terms[walker], preferred_element_type=jnp.float32) / order
                for walker in range(w_local)
            ]
            totals = [total + product for total, product in zip(totals, products)]
            terms = [product.astype(jnp.bfloat16) for product in products]
        for walker in range(w_local):
            out_ref[walker] = totals[walker].astype(jnp.bfloat16)

    return pl.pallas_call(
        body,
        out_shape=jax.ShapeDtypeStruct(own.shape, jnp.bfloat16),
        in_specs=[VMEM, VMEM, VMEM, VMEM, VMEM, SMEM, SMEM],
        out_specs=VMEM,
        scratch_shapes=[
            pltpu.VMEM(own.shape, jnp.bfloat16),
            pltpu.VMEM((w_local, orbitals, orbitals), jnp.bfloat16),
        ],
        compiler_params=params(16),
        name="propagate",
    )(blocks, one_body, low, own, high, src_shift, src_slot)


def plain(chol, walkers, trial, one_body, fields, src_shift, src_slot):
    count = lax.axis_size("pair")
    w_local, orbitals, _ = walkers.shape
    moved = lax.all_to_all(walkers, "pair", split_axis=1, concat_axis=0, tiled=True)
    formed = jnp.einsum("wia,ka->wik", moved, trial, preferred_element_type=jnp.float32)
    green_rows = formed.astype(jnp.bfloat16).reshape(moved.shape[0], moved.shape[1] * orbitals)
    partial_bias = lax.dot_general(
        green_rows, chol, (((1,), (1,)), ((), ())), preferred_element_type=jnp.float32
    )
    partials = exchange(partial_bias).reshape(count, w_local, -1)
    total = jnp.sum(partials, axis=0)
    shift = (fields - jnp.clip(sqrt_tau * total, -bias_cap, bias_cap)).astype(jnp.bfloat16)
    shifts = exchange(jnp.broadcast_to(shift[None], (count,) + shift.shape))
    shifts = shifts.reshape(count * w_local, -1)
    local_potential = (sqrt_tau * jnp.dot(shifts, chol, preferred_element_type=jnp.float32)).astype(
        jnp.bfloat16
    )
    own_potential = lax.all_to_all(local_potential, "pair", split_axis=0, concat_axis=1, tiled=True)
    amat = own_potential.astype(jnp.float32).reshape(w_local, orbitals, orbitals) + one_body.astype(
        jnp.float32
    )
    amat = amat.astype(jnp.bfloat16)
    term = walkers
    total = walkers.astype(jnp.float32)
    for order in range(1, TERMS):
        product = jnp.einsum("wik,wka->wia", amat, term, preferred_element_type=jnp.float32) / order
        total = total + product
        term = product.astype(jnp.bfloat16)
    propagated = total.astype(jnp.bfloat16)
    low, high = neighbours(propagated)
    position = (src_shift + 1) * w_local + src_slot
    return jnp.take(jnp.concatenate([low, propagated, high], axis=0), position, axis=0)


def held(chol, walkers, trial, one_body, fields, src_shift, src_slot):
    count = lax.axis_size("pair")
    w_local, orbitals, _ = walkers.shape

    low, high = neighbours(walkers)
    sent = pack(walkers, count)
    moved = exchange(sent)
    partial = bias_partial(moved, trial, chol, w_local)
    partials = exchange(partial)
    blocks = exchange(shift_blocks(partials, fields, src_shift, src_slot))
    received = exchange(potential(blocks, chol, w_local, orbitals))
    return propagate(received, one_body, low, walkers, high, src_shift, src_slot)


def shards(chol, walkers, *rest):
    rows = chol.shape[1] // walkers.shape[1]
    fits = 2 * chol.size <= 32 * MIB and rows % 16 == 0 and chol.shape[0] % LANES == 0
    return (held if fits else plain)(chol, walkers, *rest)


def solution(mesh):
    placed = (
        P("groups", "pair"),
        P(("groups", "pair"), None, None),
        P("groups", None),
        P("groups", None),
        P(("groups", "pair"), None),
        P(("groups", "pair")),
        P(("groups", "pair")),
    )
    return jax.shard_map(
        shards,
        mesh=mesh,
        in_specs=placed,
        out_specs=P(("groups", "pair"), None, None),
        check_vma=False,
    )
```

```python
import jax
import jax.numpy as jnp
from jax import lax
from jax.experimental import pallas as pl
from jax.experimental.pallas import tpu as pltpu
from jax.sharding import PartitionSpec as P


TERMS = 6
LANES = 128
MIB = 1 << 20
GROUP = 8
COVER = pl.CostEstimate(flops=100_000_000_000, bytes_accessed=400_000_000, transcendentals=0)

sqrt_tau = 0.1
bias_cap = 1.0

VMEM = pl.BlockSpec(memory_space=pltpu.VMEM)
SMEM = pl.BlockSpec(memory_space=pltpu.SMEM)
ANY = pl.BlockSpec(memory_space=pl.ANY)


def params(mib):
    return pltpu.CompilerParams(vmem_limit_bytes=mib * MIB)


def exchange(blocks):
    return lax.all_to_all(blocks, "pair", split_axis=0, concat_axis=0, tiled=True)


def neighbours(block):
    count = lax.axis_size("pair")
    forward = [(i, (i + 1) % count) for i in range(count)]
    backward = [(target, source) for source, target in forward]
    return lax.ppermute(block, "pair", forward), lax.ppermute(block, "pair", backward)


def pack(walkers, count):
    w_local, orbitals, occupied = walkers.shape
    rows = orbitals // count

    def body(in_ref, out_ref):
        for walker in range(w_local):
            out_ref[:, walker * rows : (walker + 1) * rows, :] = in_ref[walker].reshape(count, rows, occupied)

    return pl.pallas_call(
        body,
        out_shape=jax.ShapeDtypeStruct((count, w_local * rows, occupied), jnp.bfloat16),
        in_specs=[VMEM],
        out_specs=VMEM,
        compiler_params=params(4),
        cost_estimate=COVER,
        name="pack",
    )(walkers)


def bias_partial(moved, trial, chol, w_local):
    count, height, occupied = moved.shape
    orbitals = trial.shape[0]
    vectors, pairs = chol.shape
    rows = pairs // orbitals
    walkers = count * w_local
    strips = vectors // LANES
    steps = 2
    width = pairs // steps

    def body(moved_ref, trial_ref, chol_ref, out_ref, wide_ref, lhs_ref, green_ref, acc_ref, flat_ref):
        wide_ref[...] = moved_ref[...].astype(jnp.float32).reshape(count * height, occupied)
        for row in range(rows):
            lhs_ref[row * walkers : (row + 1) * walkers, :] = wide_ref[
                pl.ds(row, walkers, stride=rows), :
            ].astype(jnp.bfloat16)
        formed = lax.dot_general(
            lhs_ref[...], trial_ref[...], (((1,), (1,)), ((), ())), preferred_element_type=jnp.float32
        )
        for row in range(rows):
            green_ref[:, row * orbitals : (row + 1) * orbitals] = formed[
                row * walkers : (row + 1) * walkers, :
            ].astype(jnp.bfloat16)
        acc_ref[...] = jnp.zeros_like(acc_ref)

        @pl.loop(0, steps)
        def _(step):
            cols = pl.ds(pl.multiple_of(step * width, width), width)
            acc_ref[...] += lax.dot_general(
                chol_ref[:, cols], green_ref[:, cols], (((1,), (1,)), ((), ())), preferred_element_type=jnp.float32
            )

        for strip in range(strips):
            flat_ref[pl.ds(strip, walkers, stride=strips), :] = acc_ref[strip * LANES : (strip + 1) * LANES, :].T
        out_ref[...] = flat_ref[...].astype(jnp.bfloat16).reshape(out_ref.shape)

    return pl.pallas_call(
        body,
        out_shape=jax.ShapeDtypeStruct((count, w_local * strips, LANES), jnp.bfloat16),
        in_specs=[VMEM, VMEM, VMEM],
        out_specs=VMEM,
        scratch_shapes=[
            pltpu.VMEM((count * height, occupied), jnp.float32),
            pltpu.VMEM((count * height, occupied), jnp.bfloat16),
            pltpu.VMEM((walkers, pairs), jnp.bfloat16),
            pltpu.VMEM((vectors, walkers), jnp.float32),
            pltpu.VMEM((walkers * strips, LANES), jnp.float32),
        ],
        compiler_params=params(16),
        name="bias_partial",
    )(moved, trial, chol)


def shift_blocks(partials, fields, src_shift, src_slot):
    count, strips, _ = partials.shape
    w_local, vectors = fields.shape
    each = vectors // LANES

    def body(partials_ref, fields_ref, from_ref, slot_ref, out_ref, flat_ref):
        for walker in range(w_local):
            for strip in range(each):
                flat_ref[walker * each + strip, :] = fields_ref[walker, strip * LANES : (strip + 1) * LANES]
        total = jnp.sum(partials_ref[...].astype(jnp.float32), axis=0)
        shift = flat_ref[...] - jnp.clip(sqrt_tau * total, -bias_cap, bias_cap)
        lane = lax.broadcasted_iota(jnp.int32, (8, LANES), 1)
        table = jnp.zeros((8, LANES), jnp.int32)
        for walker in range(w_local):
            table = jnp.where(lane == walker, from_ref[walker], table)
            table = jnp.where(lane == w_local + walker, slot_ref[walker], table)
        block = jnp.concatenate([shift, table.astype(jnp.float32)], axis=0).astype(jnp.bfloat16)
        out_ref[...] = jnp.broadcast_to(block[None], out_ref.shape)

    return pl.pallas_call(
        body,
        out_shape=jax.ShapeDtypeStruct((count, strips + 8, LANES), jnp.bfloat16),
        in_specs=[VMEM, VMEM, SMEM, SMEM],
        out_specs=VMEM,
        scratch_shapes=[pltpu.VMEM((strips, LANES), jnp.float32)],
        compiler_params=params(4),
        cost_estimate=COVER,
        name="shift_blocks",
    )(partials, fields, src_shift, src_slot)


def parents_shift(blocks_ref, wide_ref, shift_ref, w_local, each):
    count, height, _ = blocks_ref.shape
    walkers = count * w_local
    wide_ref[...] = blocks_ref[...].astype(jnp.float32).reshape(count * height, LANES)
    for slot in range(w_local):
        for strip in range(each):
            shift_ref[slot * count : (slot + 1) * count, strip * LANES : (strip + 1) * LANES] = wide_ref[
                pl.ds(slot * each + strip, count, stride=height), :
            ].astype(jnp.bfloat16)
    table = wide_ref[pl.ds(w_local * each, count, stride=height), :]
    device = lax.broadcasted_iota(jnp.int32, (count, walkers), 0).astype(jnp.float32)
    place = lax.broadcasted_iota(jnp.int32, (count, walkers), 1).astype(jnp.float32)
    picks = []
    for slot in range(w_local):
        parent = device + table[:, slot : slot + 1]
        parent = jnp.where(parent < 0, parent + count, parent)
        parent = jnp.where(parent >= count, parent - count, parent)
        parent = parent + count * table[:, w_local + slot : w_local + slot + 1]
        picks.append(jnp.where(place == parent, 1.0, 0.0))
    pick = jnp.concatenate(picks, axis=0).astype(jnp.bfloat16)
    return jnp.dot(pick, shift_ref[...], preferred_element_type=jnp.float32).astype(jnp.bfloat16)


def spread(part, acc_ref, inner, count, w_local, group):
    for slot in range(w_local):
        for lane in range(part.shape[1] // LANES):
            acc_ref[lane, pl.ds(slot * group + inner, count, stride=w_local * group), :] = part[
                slot * count : (slot + 1) * count, lane * LANES : (lane + 1) * LANES
            ]


def potential(blocks, chol, w_local, orbitals):
    count, height, _ = blocks.shape
    vectors, pairs = chol.shape
    rows = pairs // orbitals
    walkers = count * w_local
    each = vectors // LANES
    width = GROUP * orbitals

    def body(blocks_ref, chol_ref, out_ref, wide_ref, shift_ref, picked_ref, acc_ref):
        step = pl.program_id(0)

        @pl.when(step == 0)
        def _():
            picked_ref[...] = parents_shift(blocks_ref, wide_ref, shift_ref, w_local, each)

        cols = pl.ds(pl.multiple_of(step * width, width), width)
        part = sqrt_tau * jnp.dot(picked_ref[...], chol_ref[:, cols], preferred_element_type=jnp.float32)
        for row in range(GROUP):
            spread(part[:, row * orbitals : (row + 1) * orbitals], acc_ref, row, count, w_local, GROUP)
        for lane in range(orbitals // LANES):
            out_ref[:, :, :, lane * LANES : (lane + 1) * LANES] = (
                acc_ref[lane].reshape(count, w_local, GROUP, LANES).astype(jnp.bfloat16)
            )

    out = pl.pallas_call(
        body,
        out_shape=jax.ShapeDtypeStruct((count, w_local, rows, orbitals), jnp.bfloat16),
        grid=(rows // GROUP,),
        in_specs=[VMEM, VMEM],
        out_specs=pl.BlockSpec((count, w_local, GROUP, orbitals), lambda i: (0, 0, i, 0)),
        scratch_shapes=[
            pltpu.VMEM((count * height, LANES), jnp.float32),
            pltpu.VMEM((walkers, vectors), jnp.bfloat16),
            pltpu.VMEM((walkers, vectors), jnp.bfloat16),
            pltpu.VMEM((orbitals // LANES, walkers * GROUP, LANES), jnp.float32),
        ],
        compiler_params=params(12),
        name="potential",
    )(blocks, chol)
    return out.reshape(count, w_local * rows, orbitals)


def propagate(blocks, one_body, low, own, high, src_shift, src_slot):
    w_local, orbitals, _ = own.shape
    count = blocks.shape[0]
    rows = orbitals // count

    def body(blocks_ref, one_ref, low_ref, own_ref, high_ref, from_ref, slot_ref, out_ref, term_ref, mat_ref, sems):
        def fetch(source, walker):
            return pltpu.make_async_copy(source.at[slot_ref[walker]], term_ref.at[walker], sems.at[walker])

        for walker in range(w_local):
            for offset, source in ((-1, low_ref), (0, own_ref), (1, high_ref)):

                @pl.when(from_ref[walker] == offset)
                def _():
                    fetch(source, walker).start()

        one = one_ref[...].astype(jnp.float32).reshape(count, rows, orbitals)
        for walker in range(w_local):
            mine = blocks_ref[:, walker * rows : (walker + 1) * rows, :].astype(jnp.float32)
            mat_ref[walker] = (mine + one).reshape(orbitals, orbitals).astype(jnp.bfloat16)
        for walker in range(w_local):
            fetch(own_ref, walker).wait()
        terms = [term_ref[walker] for walker in range(w_local)]
        totals = [term.astype(jnp.float32) for term in terms]
        for order in range(1, TERMS):
            products = [
                jnp.dot(mat_ref[walker], terms[walker], preferred_element_type=jnp.float32) / order
                for walker in range(w_local)
            ]
            totals = [total + product for total, product in zip(totals, products)]
            terms = [product.astype(jnp.bfloat16) for product in products]
        for walker in range(w_local):
            out_ref[walker] = totals[walker].astype(jnp.bfloat16)

    return pl.pallas_call(
        body,
        out_shape=jax.ShapeDtypeStruct(own.shape, jnp.bfloat16),
        in_specs=[VMEM, VMEM, ANY, ANY, ANY, SMEM, SMEM],
        out_specs=VMEM,
        scratch_shapes=[
            pltpu.VMEM(own.shape, jnp.bfloat16),
            pltpu.VMEM((w_local, orbitals, orbitals), jnp.bfloat16),
            pltpu.SemaphoreType.DMA((w_local,)),
        ],
        compiler_params=params(16),
        name="propagate",
    )(blocks, one_body, low, own, high, src_shift, src_slot)


def plain(chol, walkers, trial, one_body, fields, src_shift, src_slot):
    count = lax.axis_size("pair")
    w_local, orbitals, _ = walkers.shape
    moved = lax.all_to_all(walkers, "pair", split_axis=1, concat_axis=0, tiled=True)
    formed = jnp.einsum("wia,ka->wik", moved, trial, preferred_element_type=jnp.float32)
    green_rows = formed.astype(jnp.bfloat16).reshape(moved.shape[0], moved.shape[1] * orbitals)
    partial_bias = lax.dot_general(
        green_rows, chol, (((1,), (1,)), ((), ())), preferred_element_type=jnp.float32
    )
    partials = exchange(partial_bias).reshape(count, w_local, -1)
    total = jnp.sum(partials, axis=0)
    shift = (fields - jnp.clip(sqrt_tau * total, -bias_cap, bias_cap)).astype(jnp.bfloat16)
    shifts = exchange(jnp.broadcast_to(shift[None], (count,) + shift.shape))
    shifts = shifts.reshape(count * w_local, -1)
    local_potential = (sqrt_tau * jnp.dot(shifts, chol, preferred_element_type=jnp.float32)).astype(
        jnp.bfloat16
    )
    own_potential = lax.all_to_all(local_potential, "pair", split_axis=0, concat_axis=1, tiled=True)
    amat = own_potential.astype(jnp.float32).reshape(w_local, orbitals, orbitals) + one_body.astype(
        jnp.float32
    )
    amat = amat.astype(jnp.bfloat16)
    term = walkers
    total = walkers.astype(jnp.float32)
    for order in range(1, TERMS):
        product = jnp.einsum("wik,wka->wia", amat, term, preferred_element_type=jnp.float32) / order
        total = total + product
        term = product.astype(jnp.bfloat16)
    propagated = total.astype(jnp.bfloat16)
    low, high = neighbours(propagated)
    position = (src_shift + 1) * w_local + src_slot
    return jnp.take(jnp.concatenate([low, propagated, high], axis=0), position, axis=0)


def held(chol, walkers, trial, one_body, fields, src_shift, src_slot):
    count = lax.axis_size("pair")
    w_local, orbitals, _ = walkers.shape

    low, high = neighbours(walkers)
    sent = pack(walkers, count)
    moved = exchange(sent)
    partial = bias_partial(moved, trial, chol, w_local)
    partials = exchange(partial)
    blocks = exchange(shift_blocks(partials, fields, src_shift, src_slot))
    received = exchange(potential(blocks, chol, w_local, orbitals))
    return propagate(received, one_body, low, walkers, high, src_shift, src_slot)


def shards(chol, walkers, *rest):
    rows = chol.shape[1] // walkers.shape[1]
    fits = 2 * chol.size <= 32 * MIB and rows % 16 == 0 and chol.shape[0] % LANES == 0
    return (held if fits else plain)(chol, walkers, *rest)


def solution(mesh):
    placed = (
        P("groups", "pair"),
        P(("groups", "pair"), None, None),
        P("groups", None),
        P("groups", None),
        P(("groups", "pair"), None),
        P(("groups", "pair")),
        P(("groups", "pair")),
    )
    return jax.shard_map(
        shards,
        mesh=mesh,
        in_specs=placed,
        out_specs=P(("groups", "pair"), None, None),
        check_vma=False,
    )
```

```python
import jax
import jax.numpy as jnp
from jax import lax
from jax.experimental import pallas as pl
from jax.experimental.pallas import tpu as pltpu
from jax.sharding import PartitionSpec as P


TERMS = 6
LANES = 128
MIB = 1 << 20
GROUP = 8
COVER = pl.CostEstimate(flops=100_000_000_000, bytes_accessed=400_000_000, transcendentals=0)

sqrt_tau = 0.1
bias_cap = 1.0

VMEM = pl.BlockSpec(memory_space=pltpu.VMEM)
SMEM = pl.BlockSpec(memory_space=pltpu.SMEM)
ANY = pl.BlockSpec(memory_space=pl.ANY)


def params(mib):
    return pltpu.CompilerParams(vmem_limit_bytes=mib * MIB)


def exchange(blocks):
    return lax.all_to_all(blocks, "pair", split_axis=0, concat_axis=0, tiled=True)


def both_sides(block):
    count = lax.axis_size("pair")
    inner = [(i, i + 1 if i % 2 == 0 else i - 1) for i in range(count)]
    outer = [(i, (i - 1 if i % 2 == 0 else i + 1) % count) for i in range(count)]
    return lax.ppermute(block, "pair", inner), lax.ppermute(block, "pair", outer)


def neighbours(block):
    count = lax.axis_size("pair")
    forward = [(i, (i + 1) % count) for i in range(count)]
    backward = [(target, source) for source, target in forward]
    return lax.ppermute(block, "pair", forward), lax.ppermute(block, "pair", backward)


def pack(walkers, count):
    w_local, orbitals, occupied = walkers.shape
    rows = orbitals // count

    def body(in_ref, out_ref):
        for walker in range(w_local):
            out_ref[:, walker * rows : (walker + 1) * rows, :] = in_ref[walker].reshape(count, rows, occupied)

    return pl.pallas_call(
        body,
        out_shape=jax.ShapeDtypeStruct((count, w_local * rows, occupied), jnp.bfloat16),
        in_specs=[VMEM],
        out_specs=VMEM,
        compiler_params=params(4),
        cost_estimate=COVER,
        name="pack",
    )(walkers)


def bias_partial(moved, trial, chol, w_local):
    count, height, occupied = moved.shape
    orbitals = trial.shape[0]
    vectors, pairs = chol.shape
    rows = pairs // orbitals
    walkers = count * w_local
    strips = vectors // LANES
    steps = 2
    width = pairs // steps

    def body(moved_ref, trial_ref, chol_ref, out_ref, wide_ref, lhs_ref, green_ref, acc_ref, flat_ref):
        wide_ref[...] = moved_ref[...].astype(jnp.float32).reshape(count * height, occupied)
        for row in range(rows):
            lhs_ref[row * walkers : (row + 1) * walkers, :] = wide_ref[
                pl.ds(row, walkers, stride=rows), :
            ].astype(jnp.bfloat16)
        formed = lax.dot_general(
            lhs_ref[...], trial_ref[...], (((1,), (1,)), ((), ())), preferred_element_type=jnp.float32
        )
        for row in range(rows):
            green_ref[:, row * orbitals : (row + 1) * orbitals] = formed[
                row * walkers : (row + 1) * walkers, :
            ].astype(jnp.bfloat16)
        acc_ref[...] = jnp.zeros_like(acc_ref)

        @pl.loop(0, steps)
        def _(step):
            cols = pl.ds(pl.multiple_of(step * width, width), width)
            acc_ref[...] += lax.dot_general(
                chol_ref[:, cols], green_ref[:, cols], (((1,), (1,)), ((), ())), preferred_element_type=jnp.float32
            )

        for strip in range(strips):
            flat_ref[pl.ds(strip, walkers, stride=strips), :] = acc_ref[strip * LANES : (strip + 1) * LANES, :].T
        out_ref[...] = flat_ref[...].astype(jnp.bfloat16).reshape(out_ref.shape)

    return pl.pallas_call(
        body,
        out_shape=jax.ShapeDtypeStruct((count, w_local * strips, LANES), jnp.bfloat16),
        in_specs=[VMEM, VMEM, VMEM],
        out_specs=VMEM,
        scratch_shapes=[
            pltpu.VMEM((count * height, occupied), jnp.float32),
            pltpu.VMEM((count * height, occupied), jnp.bfloat16),
            pltpu.VMEM((walkers, pairs), jnp.bfloat16),
            pltpu.VMEM((vectors, walkers), jnp.float32),
            pltpu.VMEM((walkers * strips, LANES), jnp.float32),
        ],
        compiler_params=params(16),
        name="bias_partial",
    )(moved, trial, chol)


def shift_blocks(partials, fields, src_shift, src_slot):
    count, strips, _ = partials.shape
    w_local, vectors = fields.shape
    each = vectors // LANES

    def body(partials_ref, fields_ref, from_ref, slot_ref, out_ref, flat_ref):
        for walker in range(w_local):
            for strip in range(each):
                flat_ref[walker * each + strip, :] = fields_ref[walker, strip * LANES : (strip + 1) * LANES]
        total = jnp.sum(partials_ref[...].astype(jnp.float32), axis=0)
        shift = flat_ref[...] - jnp.clip(sqrt_tau * total, -bias_cap, bias_cap)
        lane = lax.broadcasted_iota(jnp.int32, (8, LANES), 1)
        table = jnp.zeros((8, LANES), jnp.int32)
        for walker in range(w_local):
            table = jnp.where(lane == walker, from_ref[walker], table)
            table = jnp.where(lane == w_local + walker, slot_ref[walker], table)
        block = jnp.concatenate([shift, table.astype(jnp.float32)], axis=0).astype(jnp.bfloat16)
        out_ref[...] = jnp.broadcast_to(block[None], out_ref.shape)

    return pl.pallas_call(
        body,
        out_shape=jax.ShapeDtypeStruct((count, strips + 8, LANES), jnp.bfloat16),
        in_specs=[VMEM, VMEM, SMEM, SMEM],
        out_specs=VMEM,
        scratch_shapes=[pltpu.VMEM((strips, LANES), jnp.float32)],
        compiler_params=params(4),
        cost_estimate=COVER,
        name="shift_blocks",
    )(partials, fields, src_shift, src_slot)


def parents_shift(blocks_ref, wide_ref, shift_ref, w_local, each):
    count, height, _ = blocks_ref.shape
    walkers = count * w_local
    wide_ref[...] = blocks_ref[...].astype(jnp.float32).reshape(count * height, LANES)
    for slot in range(w_local):
        for strip in range(each):
            shift_ref[slot * count : (slot + 1) * count, strip * LANES : (strip + 1) * LANES] = wide_ref[
                pl.ds(slot * each + strip, count, stride=height), :
            ].astype(jnp.bfloat16)
    table = wide_ref[pl.ds(w_local * each, count, stride=height), :]
    device = lax.broadcasted_iota(jnp.int32, (count, walkers), 0).astype(jnp.float32)
    place = lax.broadcasted_iota(jnp.int32, (count, walkers), 1).astype(jnp.float32)
    picks = []
    for slot in range(w_local):
        parent = device + table[:, slot : slot + 1]
        parent = jnp.where(parent < 0, parent + count, parent)
        parent = jnp.where(parent >= count, parent - count, parent)
        parent = parent + count * table[:, w_local + slot : w_local + slot + 1]
        picks.append(jnp.where(place == parent, 1.0, 0.0))
    pick = jnp.concatenate(picks, axis=0).astype(jnp.bfloat16)
    return jnp.dot(pick, shift_ref[...], preferred_element_type=jnp.float32).astype(jnp.bfloat16)


def spread(part, acc_ref, inner, count, w_local, group):
    for slot in range(w_local):
        for lane in range(part.shape[1] // LANES):
            acc_ref[lane, pl.ds(slot * group + inner, count, stride=w_local * group), :] = part[
                slot * count : (slot + 1) * count, lane * LANES : (lane + 1) * LANES
            ]


def potential(blocks, chol, w_local, orbitals):
    count, height, _ = blocks.shape
    vectors, pairs = chol.shape
    rows = pairs // orbitals
    walkers = count * w_local
    each = vectors // LANES
    width = GROUP * orbitals

    def body(blocks_ref, chol_ref, out_ref, wide_ref, shift_ref, picked_ref, acc_ref):
        step = pl.program_id(0)

        @pl.when(step == 0)
        def _():
            picked_ref[...] = parents_shift(blocks_ref, wide_ref, shift_ref, w_local, each)

        cols = pl.ds(pl.multiple_of(step * width, width), width)
        part = sqrt_tau * jnp.dot(picked_ref[...], chol_ref[:, cols], preferred_element_type=jnp.float32)
        for row in range(GROUP):
            spread(part[:, row * orbitals : (row + 1) * orbitals], acc_ref, row, count, w_local, GROUP)
        for lane in range(orbitals // LANES):
            out_ref[:, :, :, lane * LANES : (lane + 1) * LANES] = (
                acc_ref[lane].reshape(count, w_local, GROUP, LANES).astype(jnp.bfloat16)
            )

    out = pl.pallas_call(
        body,
        out_shape=jax.ShapeDtypeStruct((count, w_local, rows, orbitals), jnp.bfloat16),
        grid=(rows // GROUP,),
        in_specs=[VMEM, VMEM],
        out_specs=pl.BlockSpec((count, w_local, GROUP, orbitals), lambda i: (0, 0, i, 0)),
        scratch_shapes=[
            pltpu.VMEM((count * height, LANES), jnp.float32),
            pltpu.VMEM((walkers, vectors), jnp.bfloat16),
            pltpu.VMEM((walkers, vectors), jnp.bfloat16),
            pltpu.VMEM((orbitals // LANES, walkers * GROUP, LANES), jnp.float32),
        ],
        compiler_params=params(12),
        name="potential",
    )(blocks, chol)
    return out.reshape(count, w_local * rows, orbitals)


def propagate(blocks, one_body, inner, own, outer, src_shift, src_slot):
    w_local, orbitals, _ = own.shape
    count = blocks.shape[0]
    rows = orbitals // count

    def body(blocks_ref, one_ref, inner_ref, own_ref, outer_ref, from_ref, slot_ref, out_ref, term_ref, mat_ref, sems):
        def fetch(source, walker):
            return pltpu.make_async_copy(source.at[slot_ref[walker]], term_ref.at[walker], sems.at[walker])

        side = 1 - 2 * lax.rem(lax.axis_index("pair"), 2)
        for walker in range(w_local):
            for offset, side_ref in ((-1, outer_ref), (0, own_ref), (1, inner_ref)):

                @pl.when(from_ref[walker] * side == offset)
                def _():
                    fetch(side_ref, walker).start()

        one = one_ref[...].astype(jnp.float32).reshape(count, rows, orbitals)
        for walker in range(w_local):
            mine = blocks_ref[:, walker * rows : (walker + 1) * rows, :].astype(jnp.float32)
            mat_ref[walker] = (mine + one).reshape(orbitals, orbitals).astype(jnp.bfloat16)
        for walker in range(w_local):
            fetch(own_ref, walker).wait()
        terms = [term_ref[walker] for walker in range(w_local)]
        totals = [term.astype(jnp.float32) for term in terms]
        for order in range(1, TERMS):
            products = [
                jnp.dot(mat_ref[walker], terms[walker], preferred_element_type=jnp.float32) * (1.0 / order)
                for walker in range(w_local)
            ]
            totals = [total + product for total, product in zip(totals, products)]
            terms = [product.astype(jnp.bfloat16) for product in products]
        for walker in range(w_local):
            out_ref[walker] = totals[walker].astype(jnp.bfloat16)

    return pl.pallas_call(
        body,
        out_shape=jax.ShapeDtypeStruct(own.shape, jnp.bfloat16),
        in_specs=[VMEM, VMEM, ANY, ANY, ANY, SMEM, SMEM],
        out_specs=VMEM,
        scratch_shapes=[
            pltpu.VMEM(own.shape, jnp.bfloat16),
            pltpu.VMEM((w_local, orbitals, orbitals), jnp.bfloat16),
            pltpu.SemaphoreType.DMA((w_local,)),
        ],
        compiler_params=params(16),
        name="propagate",
    )(blocks, one_body, inner, own, outer, src_shift, src_slot)


def plain(chol, walkers, trial, one_body, fields, src_shift, src_slot):
    count = lax.axis_size("pair")
    w_local, orbitals, _ = walkers.shape
    moved = lax.all_to_all(walkers, "pair", split_axis=1, concat_axis=0, tiled=True)
    formed = jnp.einsum("wia,ka->wik", moved, trial, preferred_element_type=jnp.float32)
    green_rows = formed.astype(jnp.bfloat16).reshape(moved.shape[0], moved.shape[1] * orbitals)
    partial_bias = lax.dot_general(
        green_rows, chol, (((1,), (1,)), ((), ())), preferred_element_type=jnp.float32
    )
    partials = exchange(partial_bias).reshape(count, w_local, -1)
    total = jnp.sum(partials, axis=0)
    shift = (fields - jnp.clip(sqrt_tau * total, -bias_cap, bias_cap)).astype(jnp.bfloat16)
    shifts = exchange(jnp.broadcast_to(shift[None], (count,) + shift.shape))
    shifts = shifts.reshape(count * w_local, -1)
    local_potential = (sqrt_tau * jnp.dot(shifts, chol, preferred_element_type=jnp.float32)).astype(
        jnp.bfloat16
    )
    own_potential = lax.all_to_all(local_potential, "pair", split_axis=0, concat_axis=1, tiled=True)
    amat = own_potential.astype(jnp.float32).reshape(w_local, orbitals, orbitals) + one_body.astype(
        jnp.float32
    )
    amat = amat.astype(jnp.bfloat16)
    term = walkers
    total = walkers.astype(jnp.float32)
    for order in range(1, TERMS):
        product = jnp.einsum("wik,wka->wia", amat, term, preferred_element_type=jnp.float32) / order
        total = total + product
        term = product.astype(jnp.bfloat16)
    propagated = total.astype(jnp.bfloat16)
    low, high = neighbours(propagated)
    position = (src_shift + 1) * w_local + src_slot
    return jnp.take(jnp.concatenate([low, propagated, high], axis=0), position, axis=0)


def held(chol, walkers, trial, one_body, fields, src_shift, src_slot):
    count = lax.axis_size("pair")
    w_local, orbitals, _ = walkers.shape

    inner, outer = both_sides(walkers)
    sent = pack(walkers, count)
    moved = exchange(sent)
    partial = bias_partial(moved, trial, chol, w_local)
    partials = exchange(partial)
    blocks = exchange(shift_blocks(partials, fields, src_shift, src_slot))
    received = exchange(potential(blocks, chol, w_local, orbitals))
    return propagate(received, one_body, inner, walkers, outer, src_shift, src_slot)


def shards(chol, walkers, *rest):
    rows = chol.shape[1] // walkers.shape[1]
    fits = 2 * chol.size <= 32 * MIB and rows % 16 == 0 and chol.shape[0] % LANES == 0
    fits = fits and lax.axis_size("pair") % 2 == 0
    return (held if fits else plain)(chol, walkers, *rest)


def solution(mesh):
    placed = (
        P("groups", "pair"),
        P(("groups", "pair"), None, None),
        P("groups", None),
        P("groups", None),
        P(("groups", "pair"), None),
        P(("groups", "pair")),
        P(("groups", "pair")),
    )
    return jax.shard_map(
        shards,
        mesh=mesh,
        in_specs=placed,
        out_specs=P(("groups", "pair"), None, None),
        check_vma=False,
    )
```

```python
import jax
import jax.numpy as jnp
from jax import lax
from jax.experimental import pallas as pl
from jax.experimental.pallas import tpu as pltpu
from jax.sharding import PartitionSpec as P


TERMS = 6
LANES = 128
MIB = 1 << 20
GROUP = 8
COVER = pl.CostEstimate(flops=200_000_000_000, bytes_accessed=200_000_000, transcendentals=0)

sqrt_tau = 0.1
bias_cap = 1.0

VMEM = pl.BlockSpec(memory_space=pltpu.VMEM)
SMEM = pl.BlockSpec(memory_space=pltpu.SMEM)
ANY = pl.BlockSpec(memory_space=pl.ANY)


def params(mib):
    return pltpu.CompilerParams(vmem_limit_bytes=mib * MIB)


def exchange(blocks):
    return lax.all_to_all(blocks, "pair", split_axis=0, concat_axis=0, tiled=True)


def both_sides(block):
    count = lax.axis_size("pair")
    inner = [(i, i + 1 if i % 2 == 0 else i - 1) for i in range(count)]
    outer = [(i, (i - 1 if i % 2 == 0 else i + 1) % count) for i in range(count)]
    return lax.ppermute(block, "pair", inner), lax.ppermute(block, "pair", outer)


def neighbours(block):
    count = lax.axis_size("pair")
    forward = [(i, (i + 1) % count) for i in range(count)]
    backward = [(target, source) for source, target in forward]
    return lax.ppermute(block, "pair", forward), lax.ppermute(block, "pair", backward)


def pack(walkers, count):
    w_local, orbitals, occupied = walkers.shape
    rows = orbitals // count

    def body(in_ref, out_ref):
        for walker in range(w_local):
            out_ref[:, walker * rows : (walker + 1) * rows, :] = in_ref[walker].reshape(count, rows, occupied)

    return pl.pallas_call(
        body,
        out_shape=jax.ShapeDtypeStruct((count, w_local * rows, occupied), jnp.bfloat16),
        in_specs=[VMEM],
        out_specs=VMEM,
        compiler_params=params(4),
        name="pack",
    )(walkers)


def fold(chol, trial, vectors):
    orbitals, occupied = trial.shape
    rows = chol.shape[1] // orbitals
    per = 4

    def body(chol_ref, trial_ref, folded_ref):
        for row in range(per):
            folded_ref[:, row * occupied : (row + 1) * occupied] = jnp.dot(
                chol_ref[:, row * orbitals : (row + 1) * orbitals],
                trial_ref[...],
                preferred_element_type=jnp.float32,
            ).astype(jnp.bfloat16)

    return pl.pallas_call(
        body,
        out_shape=pltpu.HBM((vectors, rows * occupied), jnp.bfloat16),
        grid=(rows // per,),
        in_specs=[
            pl.BlockSpec((vectors, per * orbitals), lambda i: (0, i)),
            pl.BlockSpec((orbitals, occupied), lambda i: (0, 0)),
        ],
        out_specs=pl.BlockSpec((vectors, per * occupied), lambda i: (0, i)),
        compiler_params=params(16),
        cost_estimate=pl.CostEstimate(
            flops=2 * vectors * rows * orbitals * occupied,
            bytes_accessed=2 * vectors * rows * orbitals,
            transcendentals=0,
        ),
        name="fold",
    )(pltpu.with_memory_space_constraint(chol, pltpu.HBM), trial)


def bias_partial(moved, trial, folded, chol, w_local):
    count, height, occupied = moved.shape
    orbitals = trial.shape[0]
    vectors, pairs = chol.shape
    ready = folded.shape[0]
    rows = pairs // orbitals
    walkers = count * w_local
    strips = vectors // LANES
    steps = 4
    width = pairs // steps

    def body(moved_ref, trial_ref, folded_ref, chol_ref, out_ref, *scratch):
        wide_ref, lhs_ref, flat_lhs_ref, green_ref, folded_held_ref, chol_held_ref, flat_ref, sems = scratch
        fetch = pltpu.make_async_copy(folded_ref, folded_held_ref, sems.at[steps])
        fetch.start()

        def part_of(step):
            cols = pl.ds(step * width, width)
            return pltpu.make_async_copy(
                chol_ref.at[pl.ds(ready, vectors - ready), cols], chol_held_ref.at[:, cols], sems.at[step]
            )

        for step in range(steps):
            part_of(step).start()

        def place(sums, first):
            for strip in range(sums.shape[0] // LANES):
                flat_ref[pl.ds(first + strip, walkers, stride=strips), :] = sums[
                    strip * LANES : (strip + 1) * LANES, :
                ].T

        wide_ref[...] = moved_ref[...].astype(jnp.float32).reshape(count * height, occupied)
        for row in range(rows):
            mine = wide_ref[pl.ds(row, walkers, stride=rows), :].astype(jnp.bfloat16)
            lhs_ref[row * walkers : (row + 1) * walkers, :] = mine
            flat_lhs_ref[:, row * occupied : (row + 1) * occupied] = mine
        formed = lax.dot_general(
            lhs_ref[...], trial_ref[...], (((1,), (1,)), ((), ())), preferred_element_type=jnp.float32
        )
        for row in range(rows):
            green_ref[:, row * orbitals : (row + 1) * orbitals] = formed[
                row * walkers : (row + 1) * walkers, :
            ].astype(jnp.bfloat16)
        fetch.wait()
        place(
            lax.dot_general(
                folded_held_ref[...], flat_lhs_ref[...], (((1,), (1,)), ((), ())), preferred_element_type=jnp.float32
            ),
            0,
        )
        sums = jnp.zeros((vectors - ready, walkers), jnp.float32)
        for step in range(steps):
            part_of(step).wait()
            cols = slice(step * width, (step + 1) * width)
            sums = sums + lax.dot_general(
                chol_held_ref[:, cols], green_ref[:, cols], (((1,), (1,)), ((), ())), preferred_element_type=jnp.float32
            )
        place(sums, ready // LANES)
        out_ref[...] = flat_ref[...].astype(jnp.bfloat16).reshape(out_ref.shape)

    return pl.pallas_call(
        body,
        out_shape=jax.ShapeDtypeStruct((count, w_local * strips, LANES), jnp.bfloat16),
        in_specs=[VMEM, VMEM, ANY, ANY],
        out_specs=VMEM,
        scratch_shapes=[
            pltpu.VMEM((count * height, occupied), jnp.float32),
            pltpu.VMEM((count * height, occupied), jnp.bfloat16),
            pltpu.VMEM((walkers, rows * occupied), jnp.bfloat16),
            pltpu.VMEM((walkers, pairs), jnp.bfloat16),
            pltpu.VMEM(folded.shape, jnp.bfloat16),
            pltpu.VMEM((vectors - ready, pairs), jnp.bfloat16),
            pltpu.VMEM((walkers * strips, LANES), jnp.float32),
            pltpu.SemaphoreType.DMA((steps + 1,)),
        ],
        compiler_params=params(26),
        name="bias_partial",
    )(
        moved,
        trial,
        pltpu.with_memory_space_constraint(folded, pltpu.HBM),
        pltpu.with_memory_space_constraint(chol, pltpu.HBM),
    )


def shift_blocks(partials, fields, src_shift, src_slot):
    count, strips, _ = partials.shape
    w_local, vectors = fields.shape
    each = vectors // LANES

    def body(partials_ref, fields_ref, from_ref, slot_ref, out_ref, flat_ref):
        for walker in range(w_local):
            for strip in range(each):
                flat_ref[walker * each + strip, :] = fields_ref[walker, strip * LANES : (strip + 1) * LANES]
        total = jnp.sum(partials_ref[...].astype(jnp.float32), axis=0)
        shift = flat_ref[...] - jnp.clip(sqrt_tau * total, -bias_cap, bias_cap)
        lane = lax.broadcasted_iota(jnp.int32, (8, LANES), 1)
        table = jnp.zeros((8, LANES), jnp.int32)
        for walker in range(w_local):
            table = jnp.where(lane == walker, from_ref[walker], table)
            table = jnp.where(lane == w_local + walker, slot_ref[walker], table)
        block = jnp.concatenate([shift, table.astype(jnp.float32)], axis=0).astype(jnp.bfloat16)
        out_ref[...] = jnp.broadcast_to(block[None], out_ref.shape)

    return pl.pallas_call(
        body,
        out_shape=jax.ShapeDtypeStruct((count, strips + 8, LANES), jnp.bfloat16),
        in_specs=[VMEM, VMEM, SMEM, SMEM],
        out_specs=VMEM,
        scratch_shapes=[pltpu.VMEM((strips, LANES), jnp.float32)],
        compiler_params=params(4),
        cost_estimate=COVER,
        name="shift_blocks",
    )(partials, fields, src_shift, src_slot)


def parents_shift(blocks_ref, wide_ref, shift_ref, w_local, each):
    count, height, _ = blocks_ref.shape
    walkers = count * w_local
    wide_ref[...] = blocks_ref[...].astype(jnp.float32).reshape(count * height, LANES)
    for slot in range(w_local):
        for strip in range(each):
            shift_ref[slot * count : (slot + 1) * count, strip * LANES : (strip + 1) * LANES] = wide_ref[
                pl.ds(slot * each + strip, count, stride=height), :
            ].astype(jnp.bfloat16)
    table = wide_ref[pl.ds(w_local * each, count, stride=height), :]
    device = lax.broadcasted_iota(jnp.int32, (count, walkers), 0).astype(jnp.float32)
    place = lax.broadcasted_iota(jnp.int32, (count, walkers), 1).astype(jnp.float32)
    picks = []
    for slot in range(w_local):
        parent = device + table[:, slot : slot + 1]
        parent = jnp.where(parent < 0, parent + count, parent)
        parent = jnp.where(parent >= count, parent - count, parent)
        parent = parent + count * table[:, w_local + slot : w_local + slot + 1]
        picks.append(jnp.where(place == parent, 1.0, 0.0))
    pick = jnp.concatenate(picks, axis=0).astype(jnp.bfloat16)
    return jnp.dot(pick, shift_ref[...], preferred_element_type=jnp.float32).astype(jnp.bfloat16)


def spread(part, acc_ref, inner, count, w_local, group):
    for slot in range(w_local):
        for lane in range(part.shape[1] // LANES):
            acc_ref[lane, pl.ds(slot * group + inner, count, stride=w_local * group), :] = part[
                slot * count : (slot + 1) * count, lane * LANES : (lane + 1) * LANES
            ]


def potential(blocks, chol, w_local, orbitals):
    count, height, _ = blocks.shape
    vectors, pairs = chol.shape
    rows = pairs // orbitals
    walkers = count * w_local
    each = vectors // LANES
    width = GROUP * orbitals

    def body(blocks_ref, chol_ref, out_ref, wide_ref, shift_ref, picked_ref, acc_ref):
        step = pl.program_id(0)

        @pl.when(step == 0)
        def _():
            picked_ref[...] = parents_shift(blocks_ref, wide_ref, shift_ref, w_local, each)

        cols = pl.ds(pl.multiple_of(step * width, width), width)
        part = sqrt_tau * jnp.dot(picked_ref[...], chol_ref[:, cols], preferred_element_type=jnp.float32)
        for row in range(GROUP):
            spread(part[:, row * orbitals : (row + 1) * orbitals], acc_ref, row, count, w_local, GROUP)
        for lane in range(orbitals // LANES):
            out_ref[:, :, :, lane * LANES : (lane + 1) * LANES] = (
                acc_ref[lane].reshape(count, w_local, GROUP, LANES).astype(jnp.bfloat16)
            )

    out = pl.pallas_call(
        body,
        out_shape=jax.ShapeDtypeStruct((count, w_local, rows, orbitals), jnp.bfloat16),
        grid=(rows // GROUP,),
        in_specs=[VMEM, VMEM],
        out_specs=pl.BlockSpec((count, w_local, GROUP, orbitals), lambda i: (0, 0, i, 0)),
        scratch_shapes=[
            pltpu.VMEM((count * height, LANES), jnp.float32),
            pltpu.VMEM((walkers, vectors), jnp.bfloat16),
            pltpu.VMEM((walkers, vectors), jnp.bfloat16),
            pltpu.VMEM((orbitals // LANES, walkers * GROUP, LANES), jnp.float32),
        ],
        compiler_params=params(12),
        name="potential",
    )(blocks, chol)
    return out.reshape(count, w_local * rows, orbitals)


def propagate(blocks, one_body, inner, own, outer, src_shift, src_slot):
    w_local, orbitals, _ = own.shape
    count = blocks.shape[0]
    rows = orbitals // count

    def body(blocks_ref, one_ref, inner_ref, own_ref, outer_ref, from_ref, slot_ref, out_ref, term_ref, mat_ref, sems):
        def fetch(source, walker):
            return pltpu.make_async_copy(source.at[slot_ref[walker]], term_ref.at[walker], sems.at[walker])

        side = 1 - 2 * lax.rem(lax.axis_index("pair"), 2)
        for walker in range(w_local):
            for offset, side_ref in ((-1, outer_ref), (0, own_ref), (1, inner_ref)):

                @pl.when(from_ref[walker] * side == offset)
                def _():
                    fetch(side_ref, walker).start()

        one = one_ref[...].astype(jnp.float32).reshape(count, rows, orbitals)
        for walker in range(w_local):
            mine = blocks_ref[:, walker * rows : (walker + 1) * rows, :].astype(jnp.float32)
            mat_ref[walker] = (mine + one).reshape(orbitals, orbitals).astype(jnp.bfloat16)
        for walker in range(w_local):
            fetch(own_ref, walker).wait()
        terms = [term_ref[walker] for walker in range(w_local)]
        totals = [term.astype(jnp.float32) for term in terms]
        for order in range(1, TERMS):
            products = [
                jnp.dot(mat_ref[walker], terms[walker], preferred_element_type=jnp.float32) * (1.0 / order)
                for walker in range(w_local)
            ]
            totals = [total + product for total, product in zip(totals, products)]
            terms = [product.astype(jnp.bfloat16) for product in products]
        for walker in range(w_local):
            out_ref[walker] = totals[walker].astype(jnp.bfloat16)

    return pl.pallas_call(
        body,
        out_shape=jax.ShapeDtypeStruct(own.shape, jnp.bfloat16),
        in_specs=[VMEM, VMEM, ANY, ANY, ANY, SMEM, SMEM],
        out_specs=VMEM,
        scratch_shapes=[
            pltpu.VMEM(own.shape, jnp.bfloat16),
            pltpu.VMEM((w_local, orbitals, orbitals), jnp.bfloat16),
            pltpu.SemaphoreType.DMA((w_local,)),
        ],
        compiler_params=params(16),
        name="propagate",
    )(blocks, one_body, inner, own, outer, src_shift, src_slot)


def plain(chol, walkers, trial, one_body, fields, src_shift, src_slot):
    count = lax.axis_size("pair")
    w_local, orbitals, _ = walkers.shape
    moved = lax.all_to_all(walkers, "pair", split_axis=1, concat_axis=0, tiled=True)
    formed = jnp.einsum("wia,ka->wik", moved, trial, preferred_element_type=jnp.float32)
    green_rows = formed.astype(jnp.bfloat16).reshape(moved.shape[0], moved.shape[1] * orbitals)
    partial_bias = lax.dot_general(
        green_rows, chol, (((1,), (1,)), ((), ())), preferred_element_type=jnp.float32
    )
    partials = exchange(partial_bias).reshape(count, w_local, -1)
    total = jnp.sum(partials, axis=0)
    shift = (fields - jnp.clip(sqrt_tau * total, -bias_cap, bias_cap)).astype(jnp.bfloat16)
    shifts = exchange(jnp.broadcast_to(shift[None], (count,) + shift.shape))
    shifts = shifts.reshape(count * w_local, -1)
    local_potential = (sqrt_tau * jnp.dot(shifts, chol, preferred_element_type=jnp.float32)).astype(
        jnp.bfloat16
    )
    own_potential = lax.all_to_all(local_potential, "pair", split_axis=0, concat_axis=1, tiled=True)
    amat = own_potential.astype(jnp.float32).reshape(w_local, orbitals, orbitals) + one_body.astype(
        jnp.float32
    )
    amat = amat.astype(jnp.bfloat16)
    term = walkers
    total = walkers.astype(jnp.float32)
    for order in range(1, TERMS):
        product = jnp.einsum("wik,wka->wia", amat, term, preferred_element_type=jnp.float32) / order
        total = total + product
        term = product.astype(jnp.bfloat16)
    propagated = total.astype(jnp.bfloat16)
    low, high = neighbours(propagated)
    position = (src_shift + 1) * w_local + src_slot
    return jnp.take(jnp.concatenate([low, propagated, high], axis=0), position, axis=0)


def held(chol, walkers, trial, one_body, fields, src_shift, src_slot):
    count = lax.axis_size("pair")
    w_local, orbitals, _ = walkers.shape

    inner, outer = both_sides(walkers)
    sent = pack(walkers, count)
    moved = exchange(sent)
    folded = fold(chol, trial, chol.shape[0] * 5 // 8 // LANES * LANES)
    partial = bias_partial(moved, trial, folded, chol, w_local)
    partials = exchange(partial)
    blocks = exchange(shift_blocks(partials, fields, src_shift, src_slot))
    received = exchange(potential(blocks, chol, w_local, orbitals))
    return propagate(received, one_body, inner, walkers, outer, src_shift, src_slot)


def shards(chol, walkers, *rest):
    rows = chol.shape[1] // walkers.shape[1]
    fits = 2 * chol.size <= 32 * MIB and rows % 16 == 0 and chol.shape[0] % (8 * LANES) == 0
    fits = fits and lax.axis_size("pair") % 2 == 0
    return (held if fits else plain)(chol, walkers, *rest)


def solution(mesh):
    placed = (
        P("groups", "pair"),
        P(("groups", "pair"), None, None),
        P("groups", None),
        P("groups", None),
        P(("groups", "pair"), None),
        P(("groups", "pair")),
        P(("groups", "pair")),
    )
    return jax.shard_map(
        shards,
        mesh=mesh,
        in_specs=placed,
        out_specs=P(("groups", "pair"), None, None),
        check_vma=False,
    )
```

```python
import jax
import jax.numpy as jnp
from jax import lax
from jax.experimental import pallas as pl
from jax.experimental.pallas import tpu as pltpu
from jax.sharding import PartitionSpec as P


TERMS = 6
LANES = 128
MIB = 1 << 20
GROUP = 8
TILE = 256
UNITS = 2
HELD_ROWS = 1024
COVER = pl.CostEstimate(flops=100_000_000_000, bytes_accessed=400_000_000, transcendentals=0)

sqrt_tau = 0.1
bias_cap = 1.0

VMEM = pl.BlockSpec(memory_space=pltpu.VMEM)
SMEM = pl.BlockSpec(memory_space=pltpu.SMEM)
ANY = pl.BlockSpec(memory_space=pl.ANY)


def params(mib):
    return pltpu.CompilerParams(vmem_limit_bytes=mib * MIB)


def exchange(blocks):
    return lax.all_to_all(blocks, "pair", split_axis=0, concat_axis=0, tiled=True)


def both_sides(block):
    count = lax.axis_size("pair")
    inner = [(i, i + 1 if i % 2 == 0 else i - 1) for i in range(count)]
    outer = [(i, (i - 1 if i % 2 == 0 else i + 1) % count) for i in range(count)]
    return lax.ppermute(block, "pair", inner), lax.ppermute(block, "pair", outer)


def neighbours(block):
    count = lax.axis_size("pair")
    forward = [(i, (i + 1) % count) for i in range(count)]
    backward = [(target, source) for source, target in forward]
    return lax.ppermute(block, "pair", forward), lax.ppermute(block, "pair", backward)


def pack(walkers, count):
    w_local, orbitals, occupied = walkers.shape
    rows = orbitals // count

    def body(in_ref, out_ref):
        for walker in range(w_local):
            out_ref[:, walker * rows : (walker + 1) * rows, :] = in_ref[walker].reshape(count, rows, occupied)

    return pl.pallas_call(
        body,
        out_shape=jax.ShapeDtypeStruct((count, w_local * rows, occupied), jnp.bfloat16),
        in_specs=[VMEM],
        out_specs=VMEM,
        compiler_params=params(4),
        cost_estimate=COVER,
        name="pack",
    )(walkers)


def bias_partial(moved, trial, chol, w_local):
    count, height, occupied = moved.shape
    orbitals = trial.shape[0]
    vectors, pairs = chol.shape
    rows = pairs // orbitals
    walkers = count * w_local
    strips = vectors // LANES
    streamed = vectors - TILE
    pieces = 2
    piece = streamed // pieces
    tiles = pairs // TILE
    unroll = 32 if tiles % 32 == 0 else UNITS
    tall = rows // 2 * walkers

    def body(moved_ref, trial_ref, chol_ref, out_ref, wide_ref, lhs_ref, green_ref, flat_ref):
        wide_ref[...] = moved_ref[...].astype(jnp.float32).reshape(count * height, occupied)
        lhs_ref[:, occupied:] = jnp.zeros((rows * walkers, TILE - occupied), jnp.bfloat16)
        for row in range(rows):
            lhs_ref[row * walkers : (row + 1) * walkers, :occupied] = wide_ref[
                pl.ds(row, walkers, stride=rows), :
            ].astype(jnp.bfloat16)

        def form(*accs):
            beside = jnp.zeros((TILE, TILE - occupied), jnp.bfloat16)
            for unit in range(UNITS):
                weights = jnp.concatenate([trial_ref[unit * TILE : (unit + 1) * TILE, :], beside], axis=1)
                pltpu.matmul_push_rhs(weights, 0, unit, transpose=True)
            for half in range(2):
                for unit in range(UNITS):
                    lhs = lhs_ref[half * tall : (half + 1) * tall, :]
                    pltpu.matmul_acc_lhs(accs[half * UNITS + unit], lhs, load_staged_rhs=None if half else 0)
            for half in range(2):
                for unit in range(UNITS):
                    formed = pltpu.matmul_pop(accs[half * UNITS + unit]).astype(jnp.bfloat16)
                    for row in range(rows // 2):
                        start = (half * rows // 2 + row) * orbitals + unit * TILE
                        green_ref[:, start : start + TILE] = formed[row * walkers : (row + 1) * walkers, :]

        pl.run_scoped(form, *[pltpu.ACC(unit)((tall, TILE), jnp.float32) for _ in range(2) for unit in range(UNITS)])
        below = jnp.zeros((TILE - walkers, TILE), jnp.bfloat16)

        def contract(*accs):
            stream_accs, weight_accs = accs[: pieces * UNITS], accs[pieces * UNITS :]

            @pl.loop(0, tiles // unroll)
            def _(step):
                def cols(tile):
                    return pl.ds(pl.multiple_of((step * unroll + tile) * TILE, TILE), TILE)

                def push_green(tile):
                    for unit in range(UNITS):
                        weights = jnp.concatenate([green_ref[:, cols(tile + unit)], below], axis=0)
                        pltpu.matmul_push_rhs(weights, 0, unit, transpose=True)

                push_green(0)
                for tile in range(0, unroll, UNITS):
                    for part in range(pieces):
                        for unit in range(UNITS):
                            pltpu.matmul_acc_lhs(
                                stream_accs[part * UNITS + unit],
                                chol_ref[part * piece : (part + 1) * piece, cols(tile + unit)],
                                load_staged_rhs=0 if part == 0 else None,
                            )
                        if part == 0:
                            for unit in range(UNITS):
                                pltpu.matmul_push_rhs(chol_ref[streamed:, cols(tile + unit)], 1, unit, transpose=True)
                    for unit in range(UNITS):
                        pltpu.matmul_acc_lhs(weight_accs[unit], green_ref[:, cols(tile + unit)], load_staged_rhs=1)
                    if tile + UNITS < unroll:
                        push_green(tile + UNITS)

            def total(refs):
                first, *others = [pltpu.matmul_pop(ref) for ref in refs]
                for other in others:
                    first = first + other
                return first

            for part in range(pieces):
                sums = total(stream_accs[part * UNITS : (part + 1) * UNITS])[:, :walkers]
                for strip in range(piece // LANES):
                    flat_ref[pl.ds(part * (piece // LANES) + strip, walkers, stride=strips), :] = sums[
                        strip * LANES : (strip + 1) * LANES, :
                    ].T
            sums = total(weight_accs)
            for strip in range(TILE // LANES):
                flat_ref[pl.ds(streamed // LANES + strip, walkers, stride=strips), :] = sums[
                    :, strip * LANES : (strip + 1) * LANES
                ]

        pl.run_scoped(
            contract,
            *[pltpu.ACC(unit)((piece, TILE), jnp.float32) for _ in range(pieces) for unit in range(UNITS)],
            *[pltpu.ACC(unit)((walkers, TILE), jnp.float32) for unit in range(UNITS)],
        )
        out_ref[...] = flat_ref[...].astype(jnp.bfloat16).reshape(out_ref.shape)

    return pl.pallas_call(
        body,
        out_shape=jax.ShapeDtypeStruct((count, w_local * strips, LANES), jnp.bfloat16),
        in_specs=[VMEM, VMEM, VMEM],
        out_specs=VMEM,
        scratch_shapes=[
            pltpu.VMEM((count * height, occupied), jnp.float32),
            pltpu.VMEM((rows * walkers, TILE), jnp.bfloat16),
            pltpu.VMEM((walkers, pairs), jnp.bfloat16),
            pltpu.VMEM((walkers * strips, LANES), jnp.float32),
        ],
        compiler_params=params(16),
        name="bias_partial",
    )(moved, trial, chol)


def shift_blocks(partials, fields, src_shift, src_slot):
    count, strips, _ = partials.shape
    w_local, vectors = fields.shape
    each = vectors // LANES

    def body(partials_ref, fields_ref, from_ref, slot_ref, out_ref, flat_ref):
        for walker in range(w_local):
            for strip in range(each):
                flat_ref[walker * each + strip, :] = fields_ref[walker, strip * LANES : (strip + 1) * LANES]
        total = jnp.sum(partials_ref[...].astype(jnp.float32), axis=0)
        shift = flat_ref[...] - jnp.clip(sqrt_tau * total, -bias_cap, bias_cap)
        lane = lax.broadcasted_iota(jnp.int32, (8, LANES), 1)
        table = jnp.zeros((8, LANES), jnp.int32)
        for walker in range(w_local):
            table = jnp.where(lane == walker, from_ref[walker], table)
            table = jnp.where(lane == w_local + walker, slot_ref[walker], table)
        block = jnp.concatenate([shift, table.astype(jnp.float32)], axis=0).astype(jnp.bfloat16)
        out_ref[...] = jnp.broadcast_to(block[None], out_ref.shape)

    return pl.pallas_call(
        body,
        out_shape=jax.ShapeDtypeStruct((count, strips + 8, LANES), jnp.bfloat16),
        in_specs=[VMEM, VMEM, SMEM, SMEM],
        out_specs=VMEM,
        scratch_shapes=[pltpu.VMEM((strips, LANES), jnp.float32)],
        compiler_params=params(4),
        cost_estimate=COVER,
        name="shift_blocks",
    )(partials, fields, src_shift, src_slot)


def parents_shift(blocks_ref, wide_ref, shift_ref, w_local, each):
    count, height, _ = blocks_ref.shape
    walkers = count * w_local
    wide_ref[...] = blocks_ref[...].astype(jnp.float32).reshape(count * height, LANES)
    for slot in range(w_local):
        for strip in range(each):
            shift_ref[slot * count : (slot + 1) * count, strip * LANES : (strip + 1) * LANES] = wide_ref[
                pl.ds(slot * each + strip, count, stride=height), :
            ].astype(jnp.bfloat16)
    table = wide_ref[pl.ds(w_local * each, count, stride=height), :]
    device = lax.broadcasted_iota(jnp.int32, (count, walkers), 0).astype(jnp.float32)
    place = lax.broadcasted_iota(jnp.int32, (count, walkers), 1).astype(jnp.float32)
    picks = []
    for slot in range(w_local):
        parent = device + table[:, slot : slot + 1]
        parent = jnp.where(parent < 0, parent + count, parent)
        parent = jnp.where(parent >= count, parent - count, parent)
        parent = parent + count * table[:, w_local + slot : w_local + slot + 1]
        picks.append(jnp.where(place == parent, 1.0, 0.0))
    pick = jnp.concatenate(picks, axis=0).astype(jnp.bfloat16)
    return jnp.dot(pick, shift_ref[...], preferred_element_type=jnp.float32).astype(jnp.bfloat16)


def spread(part, acc_ref, inner, count, w_local, group):
    for slot in range(w_local):
        for lane in range(part.shape[1] // LANES):
            acc_ref[lane, pl.ds(slot * group + inner, count, stride=w_local * group), :] = part[
                slot * count : (slot + 1) * count, lane * LANES : (lane + 1) * LANES
            ]


def potential(blocks, chol, w_local, orbitals):
    count, height, _ = blocks.shape
    vectors, pairs = chol.shape
    rows = pairs // orbitals
    walkers = count * w_local
    each = vectors // LANES
    width = GROUP * orbitals

    def body(blocks_ref, chol_ref, out_ref, wide_ref, shift_ref, picked_ref, acc_ref):
        step = pl.program_id(0)

        @pl.when(step == 0)
        def _():
            picked_ref[...] = parents_shift(blocks_ref, wide_ref, shift_ref, w_local, each)

        cols = pl.ds(pl.multiple_of(step * width, width), width)
        part = sqrt_tau * jnp.dot(picked_ref[...], chol_ref[:, cols], preferred_element_type=jnp.float32)
        for row in range(GROUP):
            spread(part[:, row * orbitals : (row + 1) * orbitals], acc_ref, row, count, w_local, GROUP)
        for lane in range(orbitals // LANES):
            out_ref[:, :, :, lane * LANES : (lane + 1) * LANES] = (
                acc_ref[lane].reshape(count, w_local, GROUP, LANES).astype(jnp.bfloat16)
            )

    out = pl.pallas_call(
        body,
        out_shape=jax.ShapeDtypeStruct((count, w_local, rows, orbitals), jnp.bfloat16),
        grid=(rows // GROUP,),
        in_specs=[VMEM, VMEM],
        out_specs=pl.BlockSpec((count, w_local, GROUP, orbitals), lambda i: (0, 0, i, 0)),
        scratch_shapes=[
            pltpu.VMEM((count * height, LANES), jnp.float32),
            pltpu.VMEM((walkers, vectors), jnp.bfloat16),
            pltpu.VMEM((walkers, vectors), jnp.bfloat16),
            pltpu.VMEM((orbitals // LANES, walkers * GROUP, LANES), jnp.float32),
        ],
        compiler_params=params(12),
        name="potential",
    )(blocks, chol)
    return out.reshape(count, w_local * rows, orbitals)


def propagate(blocks, one_body, inner, own, outer, src_shift, src_slot):
    w_local, orbitals, _ = own.shape
    count = blocks.shape[0]
    rows = orbitals // count

    def body(blocks_ref, one_ref, inner_ref, own_ref, outer_ref, from_ref, slot_ref, out_ref, term_ref, mat_ref, sems):
        def fetch(source, walker):
            return pltpu.make_async_copy(source.at[slot_ref[walker]], term_ref.at[walker], sems.at[walker])

        side = 1 - 2 * lax.rem(lax.axis_index("pair"), 2)
        for walker in range(w_local):
            for offset, side_ref in ((-1, outer_ref), (0, own_ref), (1, inner_ref)):

                @pl.when(from_ref[walker] * side == offset)
                def _():
                    fetch(side_ref, walker).start()

        one = one_ref[...].astype(jnp.float32).reshape(count, rows, orbitals)
        for walker in range(w_local):
            mine = blocks_ref[:, walker * rows : (walker + 1) * rows, :].astype(jnp.float32)
            mat_ref[walker] = (mine + one).reshape(orbitals, orbitals).astype(jnp.bfloat16)
        for walker in range(w_local):
            fetch(own_ref, walker).wait()
        terms = [term_ref[walker] for walker in range(w_local)]
        totals = [term.astype(jnp.float32) for term in terms]
        for order in range(1, TERMS):
            products = [
                jnp.dot(mat_ref[walker], terms[walker], preferred_element_type=jnp.float32) * (1.0 / order)
                for walker in range(w_local)
            ]
            totals = [total + product for total, product in zip(totals, products)]
            terms = [product.astype(jnp.bfloat16) for product in products]
        for walker in range(w_local):
            out_ref[walker] = totals[walker].astype(jnp.bfloat16)

    return pl.pallas_call(
        body,
        out_shape=jax.ShapeDtypeStruct(own.shape, jnp.bfloat16),
        in_specs=[VMEM, VMEM, ANY, ANY, ANY, SMEM, SMEM],
        out_specs=VMEM,
        scratch_shapes=[
            pltpu.VMEM(own.shape, jnp.bfloat16),
            pltpu.VMEM((w_local, orbitals, orbitals), jnp.bfloat16),
            pltpu.SemaphoreType.DMA((w_local,)),
        ],
        compiler_params=params(16),
        name="propagate",
    )(blocks, one_body, inner, own, outer, src_shift, src_slot)


def plain(chol, walkers, trial, one_body, fields, src_shift, src_slot):
    count = lax.axis_size("pair")
    w_local, orbitals, _ = walkers.shape
    moved = lax.all_to_all(walkers, "pair", split_axis=1, concat_axis=0, tiled=True)
    formed = jnp.einsum("wia,ka->wik", moved, trial, preferred_element_type=jnp.float32)
    green_rows = formed.astype(jnp.bfloat16).reshape(moved.shape[0], moved.shape[1] * orbitals)
    partial_bias = lax.dot_general(
        green_rows, chol, (((1,), (1,)), ((), ())), preferred_element_type=jnp.float32
    )
    partials = exchange(partial_bias).reshape(count, w_local, -1)
    total = jnp.sum(partials, axis=0)
    shift = (fields - jnp.clip(sqrt_tau * total, -bias_cap, bias_cap)).astype(jnp.bfloat16)
    shifts = exchange(jnp.broadcast_to(shift[None], (count,) + shift.shape))
    shifts = shifts.reshape(count * w_local, -1)
    local_potential = (sqrt_tau * jnp.dot(shifts, chol, preferred_element_type=jnp.float32)).astype(
        jnp.bfloat16
    )
    own_potential = lax.all_to_all(local_potential, "pair", split_axis=0, concat_axis=1, tiled=True)
    amat = own_potential.astype(jnp.float32).reshape(w_local, orbitals, orbitals) + one_body.astype(
        jnp.float32
    )
    amat = amat.astype(jnp.bfloat16)
    term = walkers
    total = walkers.astype(jnp.float32)
    for order in range(1, TERMS):
        product = jnp.einsum("wik,wka->wia", amat, term, preferred_element_type=jnp.float32) / order
        total = total + product
        term = product.astype(jnp.bfloat16)
    propagated = total.astype(jnp.bfloat16)
    low, high = neighbours(propagated)
    position = (src_shift + 1) * w_local + src_slot
    return jnp.take(jnp.concatenate([low, propagated, high], axis=0), position, axis=0)


def held(chol, walkers, trial, one_body, fields, src_shift, src_slot):
    count = lax.axis_size("pair")
    w_local, orbitals, _ = walkers.shape

    inner, outer = both_sides(walkers)
    sent = pack(walkers, count)
    moved = exchange(sent)
    partial = bias_partial(moved, trial, chol, w_local)
    partials = exchange(partial)
    blocks = exchange(shift_blocks(partials, fields, src_shift, src_slot))
    received = exchange(potential(blocks, chol, w_local, orbitals))
    return propagate(received, one_body, inner, walkers, outer, src_shift, src_slot)


def shards(chol, walkers, *rest):
    rows = chol.shape[1] // walkers.shape[1]
    fits = 2 * chol.size <= 32 * MIB and rows % 16 == 0 and chol.shape[0] % LANES == 0
    walkers_all = walkers.shape[0] * lax.axis_size("pair")
    fits = fits and lax.axis_size("pair") % 2 == 0 and walkers_all % 16 == 0 and walkers_all < TILE
    fits = fits and chol.shape[1] % (UNITS * TILE) == 0 and chol.shape[0] % TILE == 0
    fits = fits and walkers.shape[1] == UNITS * TILE and walkers.shape[2] < TILE
    fits = fits and rows * walkers_all <= HELD_ROWS
    fits = fits and TILE < chol.shape[0] and chol.shape[0] - TILE + walkers_all <= HELD_ROWS
    return (held if fits else plain)(chol, walkers, *rest)


def solution(mesh):
    placed = (
        P("groups", "pair"),
        P(("groups", "pair"), None, None),
        P("groups", None),
        P("groups", None),
        P(("groups", "pair"), None),
        P(("groups", "pair")),
        P(("groups", "pair")),
    )
    return jax.shard_map(
        shards,
        mesh=mesh,
        in_specs=placed,
        out_specs=P(("groups", "pair"), None, None),
        check_vma=False,
    )
```

```python
import jax
import jax.numpy as jnp
from jax import lax
from jax.experimental import pallas as pl
from jax.experimental.pallas import tpu as pltpu
from jax.sharding import PartitionSpec as P


TERMS = 6
LANES = 128
MIB = 1 << 20
GROUP = 16
TILE = 256
UNITS = 2
HELD_ROWS = 1024
COVER = pl.CostEstimate(flops=100_000_000_000, bytes_accessed=400_000_000, transcendentals=0)

sqrt_tau = 0.1
bias_cap = 1.0

VMEM = pl.BlockSpec(memory_space=pltpu.VMEM)
SMEM = pl.BlockSpec(memory_space=pltpu.SMEM)
ANY = pl.BlockSpec(memory_space=pl.ANY)


def params(mib):
    return pltpu.CompilerParams(vmem_limit_bytes=mib * MIB)


def exchange(blocks):
    return lax.all_to_all(blocks, "pair", split_axis=0, concat_axis=0, tiled=True)


def partners(count):
    inner = [(i, i + 1 if i % 2 == 0 else i - 1) for i in range(count)]
    outer = [(i, (i - 1 if i % 2 == 0 else i + 1) % count) for i in range(count)]
    return inner, outer


def neighbours(block):
    count = lax.axis_size("pair")
    forward = [(i, (i + 1) % count) for i in range(count)]
    backward = [(target, source) for source, target in forward]
    return lax.ppermute(block, "pair", forward), lax.ppermute(block, "pair", backward)


def pack(walkers, count):
    w_local, orbitals, occupied = walkers.shape
    rows = orbitals // count

    def body(in_ref, out_ref):
        for walker in range(w_local):
            out_ref[:, walker * rows : (walker + 1) * rows, :] = in_ref[walker].reshape(count, rows, occupied)

    return pl.pallas_call(
        body,
        out_shape=jax.ShapeDtypeStruct((count, w_local * rows, occupied), jnp.bfloat16),
        in_specs=[VMEM],
        out_specs=VMEM,
        compiler_params=params(4),
        cost_estimate=COVER,
        name="pack",
    )(walkers)


def bias_partial(moved, trial, chol, w_local):
    count, height, occupied = moved.shape
    orbitals = trial.shape[0]
    vectors, pairs = chol.shape
    rows = pairs // orbitals
    walkers = count * w_local
    strips = vectors // LANES
    streamed = vectors - TILE
    pieces = 2
    piece = streamed // pieces
    tiles = pairs // TILE
    unroll = 32 if tiles % 32 == 0 else UNITS
    tall = rows // 2 * walkers

    def body(moved_ref, trial_ref, chol_ref, out_ref, wide_ref, lhs_ref, green_ref, flat_ref):
        wide_ref[...] = moved_ref[...].astype(jnp.float32).reshape(count * height, occupied)
        lhs_ref[:, occupied:] = jnp.zeros((rows * walkers, TILE - occupied), jnp.bfloat16)
        for row in range(rows):
            lhs_ref[row * walkers : (row + 1) * walkers, :occupied] = wide_ref[
                pl.ds(row, walkers, stride=rows), :
            ].astype(jnp.bfloat16)

        def form(*accs):
            beside = jnp.zeros((TILE, TILE - occupied), jnp.bfloat16)
            for unit in range(UNITS):
                weights = jnp.concatenate([trial_ref[unit * TILE : (unit + 1) * TILE, :], beside], axis=1)
                pltpu.matmul_push_rhs(weights, 0, unit, transpose=True)
            for half in range(2):
                for unit in range(UNITS):
                    lhs = lhs_ref[half * tall : (half + 1) * tall, :]
                    pltpu.matmul_acc_lhs(accs[half * UNITS + unit], lhs, load_staged_rhs=None if half else 0)
            for half in range(2):
                for unit in range(UNITS):
                    formed = pltpu.matmul_pop(accs[half * UNITS + unit]).astype(jnp.bfloat16)
                    for row in range(rows // 2):
                        start = (half * rows // 2 + row) * orbitals + unit * TILE
                        green_ref[:, start : start + TILE] = formed[row * walkers : (row + 1) * walkers, :]

        pl.run_scoped(form, *[pltpu.ACC(unit)((tall, TILE), jnp.float32) for _ in range(2) for unit in range(UNITS)])
        below = jnp.zeros((TILE - walkers, TILE), jnp.bfloat16)

        def contract(*accs):
            stream_accs, weight_accs = accs[: pieces * UNITS], accs[pieces * UNITS :]

            @pl.loop(0, tiles // unroll)
            def _(step):
                def cols(tile):
                    return pl.ds(pl.multiple_of((step * unroll + tile) * TILE, TILE), TILE)

                def push_green(tile):
                    for unit in range(UNITS):
                        weights = jnp.concatenate([green_ref[:, cols(tile + unit)], below], axis=0)
                        pltpu.matmul_push_rhs(weights, 0, unit, transpose=True)

                push_green(0)
                for tile in range(0, unroll, UNITS):
                    for part in range(pieces):
                        for unit in range(UNITS):
                            pltpu.matmul_acc_lhs(
                                stream_accs[part * UNITS + unit],
                                chol_ref[part * piece : (part + 1) * piece, cols(tile + unit)],
                                load_staged_rhs=0 if part == 0 else None,
                            )
                        if part == 0:
                            for unit in range(UNITS):
                                pltpu.matmul_push_rhs(chol_ref[streamed:, cols(tile + unit)], 1, unit, transpose=True)
                    for unit in range(UNITS):
                        pltpu.matmul_acc_lhs(weight_accs[unit], green_ref[:, cols(tile + unit)], load_staged_rhs=1)
                    if tile + UNITS < unroll:
                        push_green(tile + UNITS)

            def total(refs):
                first, *others = [pltpu.matmul_pop(ref) for ref in refs]
                for other in others:
                    first = first + other
                return first

            for part in range(pieces):
                sums = total(stream_accs[part * UNITS : (part + 1) * UNITS])[:, :walkers]
                for strip in range(piece // LANES):
                    flat_ref[pl.ds(part * (piece // LANES) + strip, walkers, stride=strips), :] = sums[
                        strip * LANES : (strip + 1) * LANES, :
                    ].T
            sums = total(weight_accs)
            for strip in range(TILE // LANES):
                flat_ref[pl.ds(streamed // LANES + strip, walkers, stride=strips), :] = sums[
                    :, strip * LANES : (strip + 1) * LANES
                ]

        pl.run_scoped(
            contract,
            *[pltpu.ACC(unit)((piece, TILE), jnp.float32) for _ in range(pieces) for unit in range(UNITS)],
            *[pltpu.ACC(unit)((walkers, TILE), jnp.float32) for unit in range(UNITS)],
        )
        out_ref[...] = flat_ref[...].astype(jnp.bfloat16).reshape(out_ref.shape)

    return pl.pallas_call(
        body,
        out_shape=jax.ShapeDtypeStruct((count, w_local * strips, LANES), jnp.bfloat16),
        in_specs=[VMEM, VMEM, VMEM],
        out_specs=VMEM,
        scratch_shapes=[
            pltpu.VMEM((count * height, occupied), jnp.float32),
            pltpu.VMEM((rows * walkers, TILE), jnp.bfloat16),
            pltpu.VMEM((walkers, pairs), jnp.bfloat16),
            pltpu.VMEM((walkers * strips, LANES), jnp.float32),
        ],
        compiler_params=params(16),
        name="bias_partial",
    )(moved, trial, chol)


def shift_blocks(partials, fields, src_shift, src_slot):
    count, strips, _ = partials.shape
    w_local, vectors = fields.shape
    each = vectors // LANES

    def body(partials_ref, fields_ref, from_ref, slot_ref, out_ref, flat_ref):
        for walker in range(w_local):
            for strip in range(each):
                flat_ref[walker * each + strip, :] = fields_ref[walker, strip * LANES : (strip + 1) * LANES]
        total = jnp.sum(partials_ref[...].astype(jnp.float32), axis=0)
        shift = flat_ref[...] - jnp.clip(sqrt_tau * total, -bias_cap, bias_cap)
        lane = lax.broadcasted_iota(jnp.int32, (8, LANES), 1)
        table = jnp.zeros((8, LANES), jnp.int32)
        for walker in range(w_local):
            table = jnp.where(lane == walker, from_ref[walker], table)
            table = jnp.where(lane == w_local + walker, slot_ref[walker], table)
        block = jnp.concatenate([shift, table.astype(jnp.float32)], axis=0).astype(jnp.bfloat16)
        out_ref[...] = jnp.broadcast_to(block[None], out_ref.shape)

    return pl.pallas_call(
        body,
        out_shape=jax.ShapeDtypeStruct((count, strips + 8, LANES), jnp.bfloat16),
        in_specs=[VMEM, VMEM, SMEM, SMEM],
        out_specs=VMEM,
        scratch_shapes=[pltpu.VMEM((strips, LANES), jnp.float32)],
        compiler_params=params(4),
        cost_estimate=COVER,
        name="shift_blocks",
    )(partials, fields, src_shift, src_slot)


def parents_shift(blocks_ref, wide_ref, shift_ref, w_local, each):
    count, height, _ = blocks_ref.shape
    walkers = count * w_local
    wide_ref[...] = blocks_ref[...].astype(jnp.float32).reshape(count * height, LANES)
    for slot in range(w_local):
        for strip in range(each):
            shift_ref[slot * count : (slot + 1) * count, strip * LANES : (strip + 1) * LANES] = wide_ref[
                pl.ds(slot * each + strip, count, stride=height), :
            ].astype(jnp.bfloat16)
    table = wide_ref[pl.ds(w_local * each, count, stride=height), :]
    device = lax.broadcasted_iota(jnp.int32, (count, walkers), 0).astype(jnp.float32)
    place = lax.broadcasted_iota(jnp.int32, (count, walkers), 1).astype(jnp.float32)
    picks = []
    for slot in range(w_local):
        parent = device + table[:, slot : slot + 1]
        parent = jnp.where(parent < 0, parent + count, parent)
        parent = jnp.where(parent >= count, parent - count, parent)
        parent = parent + count * table[:, w_local + slot : w_local + slot + 1]
        picks.append(jnp.where(place == parent, 1.0, 0.0))
    pick = jnp.concatenate(picks, axis=0).astype(jnp.bfloat16)
    return jnp.dot(pick, shift_ref[...], preferred_element_type=jnp.float32).astype(jnp.bfloat16)


def spread(part, acc_ref, inner, count, w_local, group):
    for slot in range(w_local):
        for lane in range(part.shape[1] // LANES):
            acc_ref[lane, pl.ds(slot * group + inner, count, stride=w_local * group), :] = part[
                slot * count : (slot + 1) * count, lane * LANES : (lane + 1) * LANES
            ]


def potential(blocks, chol, w_local, orbitals):
    count, height, _ = blocks.shape
    vectors, pairs = chol.shape
    rows = pairs // orbitals
    walkers = count * w_local
    each = vectors // LANES
    width = GROUP * orbitals

    def body(blocks_ref, chol_ref, out_ref, wide_ref, shift_ref, picked_ref, acc_ref):
        step = pl.program_id(0)

        @pl.when(step == 0)
        def _():
            picked_ref[...] = parents_shift(blocks_ref, wide_ref, shift_ref, w_local, each)

        cols = pl.ds(pl.multiple_of(step * width, width), width)
        part = sqrt_tau * jnp.dot(picked_ref[...], chol_ref[:, cols], preferred_element_type=jnp.float32)
        for row in range(GROUP):
            spread(part[:, row * orbitals : (row + 1) * orbitals], acc_ref, row, count, w_local, GROUP)
        for lane in range(orbitals // LANES):
            out_ref[:, :, :, lane * LANES : (lane + 1) * LANES] = (
                acc_ref[lane].reshape(count, w_local, GROUP, LANES).astype(jnp.bfloat16)
            )

    out = pl.pallas_call(
        body,
        out_shape=jax.ShapeDtypeStruct((count, w_local, rows, orbitals), jnp.bfloat16),
        grid=(rows // GROUP,),
        in_specs=[VMEM, VMEM],
        out_specs=pl.BlockSpec((count, w_local, GROUP, orbitals), lambda i: (0, 0, i, 0)),
        scratch_shapes=[
            pltpu.VMEM((count * height, LANES), jnp.float32),
            pltpu.VMEM((walkers, vectors), jnp.bfloat16),
            pltpu.VMEM((walkers, vectors), jnp.bfloat16),
            pltpu.VMEM((orbitals // LANES, walkers * GROUP, LANES), jnp.float32),
        ],
        compiler_params=params(12),
        name="potential",
    )(blocks, chol)
    return out.reshape(count, w_local * rows, orbitals)


def choose_parents(inner, own, outer, src_shift, src_slot):
    def body(inner_ref, own_ref, outer_ref, from_ref, slot_ref, out_ref):
        side = 1 - 2 * lax.rem(lax.axis_index("pair"), 2)
        for walker in range(own.shape[0]):
            for offset, side_ref in ((-1, outer_ref), (0, own_ref), (1, inner_ref)):

                @pl.when(from_ref[walker] * side == offset)
                def _():
                    out_ref[walker] = side_ref[slot_ref[walker]]

    return pl.pallas_call(
        body,
        out_shape=jax.ShapeDtypeStruct(own.shape, jnp.bfloat16),
        in_specs=[VMEM, VMEM, VMEM, SMEM, SMEM],
        out_specs=VMEM,
        compiler_params=params(4),
        name="choose_parents",
    )(inner, own, outer, src_shift, src_slot)


def propagate(blocks, one_body, parents):
    w_local, orbitals, _ = parents.shape
    count = blocks.shape[0]
    rows = orbitals // count

    def body(blocks_ref, one_ref, parents_ref, out_ref, mat_ref):
        one = one_ref[...].astype(jnp.float32).reshape(count, rows, orbitals)
        for walker in range(w_local):
            mine = blocks_ref[:, walker * rows : (walker + 1) * rows, :].astype(jnp.float32)
            mat_ref[walker] = (mine + one).reshape(orbitals, orbitals).astype(jnp.bfloat16)
        terms = [parents_ref[walker] for walker in range(w_local)]
        totals = [term.astype(jnp.float32) for term in terms]
        for order in range(1, TERMS):
            products = [
                jnp.dot(mat_ref[walker], terms[walker], preferred_element_type=jnp.float32) * (1.0 / order)
                for walker in range(w_local)
            ]
            totals = [total + product for total, product in zip(totals, products)]
            terms = [product.astype(jnp.bfloat16) for product in products]
        for walker in range(w_local):
            out_ref[walker] = totals[walker].astype(jnp.bfloat16)

    return pl.pallas_call(
        body,
        out_shape=jax.ShapeDtypeStruct(parents.shape, jnp.bfloat16),
        in_specs=[VMEM, VMEM, VMEM],
        out_specs=VMEM,
        scratch_shapes=[pltpu.VMEM((w_local, orbitals, orbitals), jnp.bfloat16)],
        compiler_params=params(16),
        name="propagate",
    )(blocks, one_body, parents)


def plain(chol, walkers, trial, one_body, fields, src_shift, src_slot):
    count = lax.axis_size("pair")
    w_local, orbitals, _ = walkers.shape
    moved = lax.all_to_all(walkers, "pair", split_axis=1, concat_axis=0, tiled=True)
    formed = jnp.einsum("wia,ka->wik", moved, trial, preferred_element_type=jnp.float32)
    green_rows = formed.astype(jnp.bfloat16).reshape(moved.shape[0], moved.shape[1] * orbitals)
    partial_bias = lax.dot_general(
        green_rows, chol, (((1,), (1,)), ((), ())), preferred_element_type=jnp.float32
    )
    partials = exchange(partial_bias).reshape(count, w_local, -1)
    total = jnp.sum(partials, axis=0)
    shift = (fields - jnp.clip(sqrt_tau * total, -bias_cap, bias_cap)).astype(jnp.bfloat16)
    shifts = exchange(jnp.broadcast_to(shift[None], (count,) + shift.shape))
    shifts = shifts.reshape(count * w_local, -1)
    local_potential = (sqrt_tau * jnp.dot(shifts, chol, preferred_element_type=jnp.float32)).astype(
        jnp.bfloat16
    )
    own_potential = lax.all_to_all(local_potential, "pair", split_axis=0, concat_axis=1, tiled=True)
    amat = own_potential.astype(jnp.float32).reshape(w_local, orbitals, orbitals) + one_body.astype(
        jnp.float32
    )
    amat = amat.astype(jnp.bfloat16)
    term = walkers
    total = walkers.astype(jnp.float32)
    for order in range(1, TERMS):
        product = jnp.einsum("wik,wka->wia", amat, term, preferred_element_type=jnp.float32) / order
        total = total + product
        term = product.astype(jnp.bfloat16)
    propagated = total.astype(jnp.bfloat16)
    low, high = neighbours(propagated)
    position = (src_shift + 1) * w_local + src_slot
    return jnp.take(jnp.concatenate([low, propagated, high], axis=0), position, axis=0)


def held(chol, walkers, trial, one_body, fields, src_shift, src_slot):
    count = lax.axis_size("pair")
    w_local, orbitals, _ = walkers.shape

    inner_pairs, outer_pairs = partners(count)
    outer = lax.ppermute(walkers, "pair", outer_pairs)
    inner = lax.ppermute(walkers, "pair", inner_pairs)
    sent = pack(walkers, count)
    moved = exchange(sent)
    partial = bias_partial(moved, trial, chol, w_local)
    partials = exchange(partial)
    blocks = exchange(shift_blocks(partials, fields, src_shift, src_slot))
    sent = potential(blocks, chol, w_local, orbitals)
    received = exchange(sent)
    chosen = choose_parents(inner, walkers, outer, src_shift, src_slot)
    return propagate(received, one_body, chosen)


def shards(chol, walkers, *rest):
    rows = chol.shape[1] // walkers.shape[1]
    fits = 2 * chol.size <= 32 * MIB and rows % 16 == 0 and chol.shape[0] % LANES == 0
    walkers_all = walkers.shape[0] * lax.axis_size("pair")
    fits = fits and lax.axis_size("pair") % 2 == 0 and walkers_all % 16 == 0 and walkers_all < TILE
    fits = fits and chol.shape[1] % (UNITS * TILE) == 0 and chol.shape[0] % TILE == 0
    fits = fits and walkers.shape[1] == UNITS * TILE and walkers.shape[2] < TILE
    fits = fits and rows * walkers_all <= HELD_ROWS
    fits = fits and TILE < chol.shape[0] and chol.shape[0] - TILE + walkers_all <= HELD_ROWS
    return (held if fits else plain)(chol, walkers, *rest)


def solution(mesh):
    placed = (
        P("groups", "pair"),
        P(("groups", "pair"), None, None),
        P("groups", None),
        P("groups", None),
        P(("groups", "pair"), None),
        P(("groups", "pair")),
        P(("groups", "pair")),
    )
    return jax.shard_map(
        shards,
        mesh=mesh,
        in_specs=placed,
        out_specs=P(("groups", "pair"), None, None),
        check_vma=False,
    )
```

```python
import jax
import jax.numpy as jnp
from jax import lax
from jax.experimental import pallas as pl
from jax.experimental.pallas import tpu as pltpu
from jax.sharding import PartitionSpec as P


TERMS = 6
LANES = 128
MIB = 1 << 20
GROUP = 8
TILE = 256
UNITS = 2
HELD_ROWS = 1024
COVER = pl.CostEstimate(flops=100_000_000_000, bytes_accessed=400_000_000, transcendentals=0)

sqrt_tau = 0.1
bias_cap = 1.0

VMEM = pl.BlockSpec(memory_space=pltpu.VMEM)
SMEM = pl.BlockSpec(memory_space=pltpu.SMEM)
ANY = pl.BlockSpec(memory_space=pl.ANY)


def params(mib):
    return pltpu.CompilerParams(vmem_limit_bytes=mib * MIB)


def exchange(blocks):
    return lax.all_to_all(blocks, "pair", split_axis=0, concat_axis=0, tiled=True)


def partners(count):
    inner = [(i, i + 1 if i % 2 == 0 else i - 1) for i in range(count)]
    outer = [(i, (i - 1 if i % 2 == 0 else i + 1) % count) for i in range(count)]
    return inner, outer


def neighbours(block):
    count = lax.axis_size("pair")
    forward = [(i, (i + 1) % count) for i in range(count)]
    backward = [(target, source) for source, target in forward]
    return lax.ppermute(block, "pair", forward), lax.ppermute(block, "pair", backward)


def pack(walkers, count):
    w_local, orbitals, occupied = walkers.shape
    rows = orbitals // count

    def body(in_ref, out_ref):
        for walker in range(w_local):
            out_ref[:, walker * rows : (walker + 1) * rows, :] = in_ref[walker].reshape(count, rows, occupied)

    return pl.pallas_call(
        body,
        out_shape=jax.ShapeDtypeStruct((count, w_local * rows, occupied), jnp.bfloat16),
        in_specs=[VMEM],
        out_specs=VMEM,
        compiler_params=params(4),
        cost_estimate=COVER,
        name="pack",
    )(walkers)


def bias_partial(moved, trial, chol, w_local):
    count, height, occupied = moved.shape
    orbitals = trial.shape[0]
    vectors, pairs = chol.shape
    rows = pairs // orbitals
    walkers = count * w_local
    strips = vectors // LANES
    streamed = vectors - TILE
    pieces = 2
    piece = streamed // pieces
    tiles = pairs // TILE
    unroll = 32 if tiles % 32 == 0 else UNITS
    tall = rows // 2 * walkers

    def body(moved_ref, trial_ref, chol_ref, out_ref, wide_ref, lhs_ref, green_ref, flat_ref):
        wide_ref[...] = moved_ref[...].astype(jnp.float32).reshape(count * height, occupied)
        lhs_ref[:, occupied:] = jnp.zeros((rows * walkers, TILE - occupied), jnp.bfloat16)
        for row in range(rows):
            lhs_ref[row * walkers : (row + 1) * walkers, :occupied] = wide_ref[
                pl.ds(row, walkers, stride=rows), :
            ].astype(jnp.bfloat16)

        def form(*accs):
            beside = jnp.zeros((TILE, TILE - occupied), jnp.bfloat16)
            for unit in range(UNITS):
                weights = jnp.concatenate([trial_ref[unit * TILE : (unit + 1) * TILE, :], beside], axis=1)
                pltpu.matmul_push_rhs(weights, 0, unit, transpose=True)
            for half in range(2):
                for unit in range(UNITS):
                    lhs = lhs_ref[half * tall : (half + 1) * tall, :]
                    pltpu.matmul_acc_lhs(accs[half * UNITS + unit], lhs, load_staged_rhs=None if half else 0)
            for half in range(2):
                for unit in range(UNITS):
                    formed = pltpu.matmul_pop(accs[half * UNITS + unit]).astype(jnp.bfloat16)
                    for row in range(rows // 2):
                        start = (half * rows // 2 + row) * orbitals + unit * TILE
                        green_ref[:, start : start + TILE] = formed[row * walkers : (row + 1) * walkers, :]

        pl.run_scoped(form, *[pltpu.ACC(unit)((tall, TILE), jnp.float32) for _ in range(2) for unit in range(UNITS)])
        below = jnp.zeros((TILE - walkers, TILE), jnp.bfloat16)

        def contract(*accs):
            stream_accs, weight_accs = accs[: pieces * UNITS], accs[pieces * UNITS :]

            @pl.loop(0, tiles // unroll)
            def _(step):
                def cols(tile):
                    return pl.ds(pl.multiple_of((step * unroll + tile) * TILE, TILE), TILE)

                def push_green(tile):
                    for unit in range(UNITS):
                        weights = jnp.concatenate([green_ref[:, cols(tile + unit)], below], axis=0)
                        pltpu.matmul_push_rhs(weights, 0, unit, transpose=True)

                push_green(0)
                for tile in range(0, unroll, UNITS):
                    for part in range(pieces):
                        for unit in range(UNITS):
                            pltpu.matmul_acc_lhs(
                                stream_accs[part * UNITS + unit],
                                chol_ref[part * piece : (part + 1) * piece, cols(tile + unit)],
                                load_staged_rhs=0 if part == 0 else None,
                            )
                        if part == 0:
                            for unit in range(UNITS):
                                pltpu.matmul_push_rhs(chol_ref[streamed:, cols(tile + unit)], 1, unit, transpose=True)
                    for unit in range(UNITS):
                        pltpu.matmul_acc_lhs(weight_accs[unit], green_ref[:, cols(tile + unit)], load_staged_rhs=1)
                    if tile + UNITS < unroll:
                        push_green(tile + UNITS)

            def total(refs):
                first, *others = [pltpu.matmul_pop(ref) for ref in refs]
                for other in others:
                    first = first + other
                return first

            for part in range(pieces):
                sums = total(stream_accs[part * UNITS : (part + 1) * UNITS])[:, :walkers]
                for strip in range(piece // LANES):
                    flat_ref[pl.ds(part * (piece // LANES) + strip, walkers, stride=strips), :] = sums[
                        strip * LANES : (strip + 1) * LANES, :
                    ].T
            sums = total(weight_accs)
            for strip in range(TILE // LANES):
                flat_ref[pl.ds(streamed // LANES + strip, walkers, stride=strips), :] = sums[
                    :, strip * LANES : (strip + 1) * LANES
                ]

        pl.run_scoped(
            contract,
            *[pltpu.ACC(unit)((piece, TILE), jnp.float32) for _ in range(pieces) for unit in range(UNITS)],
            *[pltpu.ACC(unit)((walkers, TILE), jnp.float32) for unit in range(UNITS)],
        )
        out_ref[...] = flat_ref[...].astype(jnp.bfloat16).reshape(out_ref.shape)

    return pl.pallas_call(
        body,
        out_shape=jax.ShapeDtypeStruct((count, w_local * strips, LANES), jnp.bfloat16),
        in_specs=[VMEM, VMEM, VMEM],
        out_specs=VMEM,
        scratch_shapes=[
            pltpu.VMEM((count * height, occupied), jnp.float32),
            pltpu.VMEM((rows * walkers, TILE), jnp.bfloat16),
            pltpu.VMEM((walkers, pairs), jnp.bfloat16),
            pltpu.VMEM((walkers * strips, LANES), jnp.float32),
        ],
        compiler_params=params(16),
        name="bias_partial",
    )(moved, trial, chol)


def shift_blocks(partials, fields, src_shift, src_slot):
    count, strips, _ = partials.shape
    w_local, vectors = fields.shape
    each = vectors // LANES

    def body(partials_ref, fields_ref, from_ref, slot_ref, out_ref, flat_ref):
        for walker in range(w_local):
            for strip in range(each):
                flat_ref[walker * each + strip, :] = fields_ref[walker, strip * LANES : (strip + 1) * LANES]
        total = jnp.sum(partials_ref[...].astype(jnp.float32), axis=0)
        shift = flat_ref[...] - jnp.clip(sqrt_tau * total, -bias_cap, bias_cap)
        lane = lax.broadcasted_iota(jnp.int32, (8, LANES), 1)
        table = jnp.zeros((8, LANES), jnp.int32)
        for walker in range(w_local):
            table = jnp.where(lane == walker, from_ref[:, walker : walker + 1], table)
            table = jnp.where(lane == w_local + walker, slot_ref[:, walker : walker + 1], table)
        block = jnp.concatenate([shift, table.astype(jnp.float32)], axis=0).astype(jnp.bfloat16)
        out_ref[...] = jnp.broadcast_to(block[None], out_ref.shape)

    return pl.pallas_call(
        body,
        out_shape=jax.ShapeDtypeStruct((count, strips + 8, LANES), jnp.bfloat16),
        in_specs=[VMEM, VMEM, VMEM, VMEM],
        out_specs=VMEM,
        scratch_shapes=[pltpu.VMEM((strips, LANES), jnp.float32)],
        compiler_params=params(4),
        cost_estimate=COVER,
        name="shift_blocks",
    )(partials, fields, src_shift[None], src_slot[None])


def parents_shift(blocks_ref, wide_ref, shift_ref, w_local, each):
    count, height, _ = blocks_ref.shape
    walkers = count * w_local
    wide_ref[...] = blocks_ref[...].astype(jnp.float32).reshape(count * height, LANES)
    for slot in range(w_local):
        for strip in range(each):
            shift_ref[slot * count : (slot + 1) * count, strip * LANES : (strip + 1) * LANES] = wide_ref[
                pl.ds(slot * each + strip, count, stride=height), :
            ].astype(jnp.bfloat16)
    table = wide_ref[pl.ds(w_local * each, count, stride=height), :]
    device = lax.broadcasted_iota(jnp.int32, (count, walkers), 0).astype(jnp.float32)
    place = lax.broadcasted_iota(jnp.int32, (count, walkers), 1).astype(jnp.float32)
    picks = []
    for slot in range(w_local):
        parent = device + table[:, slot : slot + 1]
        parent = jnp.where(parent < 0, parent + count, parent)
        parent = jnp.where(parent >= count, parent - count, parent)
        parent = parent + count * table[:, w_local + slot : w_local + slot + 1]
        picks.append(jnp.where(place == parent, 1.0, 0.0))
    pick = jnp.concatenate(picks, axis=0).astype(jnp.bfloat16)
    return jnp.dot(pick, shift_ref[...], preferred_element_type=jnp.float32).astype(jnp.bfloat16)


def spread(part, acc_ref, inner, count, w_local, group):
    for slot in range(w_local):
        for lane in range(part.shape[1] // LANES):
            acc_ref[lane, pl.ds(slot * group + inner, count, stride=w_local * group), :] = part[
                slot * count : (slot + 1) * count, lane * LANES : (lane + 1) * LANES
            ]


def potential(blocks, chol, w_local, orbitals):
    count, height, _ = blocks.shape
    vectors, pairs = chol.shape
    rows = pairs // orbitals
    walkers = count * w_local
    each = vectors // LANES
    width = GROUP * orbitals

    def body(blocks_ref, chol_ref, out_ref, wide_ref, shift_ref, picked_ref, acc_ref):
        step = pl.program_id(0)

        @pl.when(step == 0)
        def _():
            picked_ref[...] = parents_shift(blocks_ref, wide_ref, shift_ref, w_local, each)

        cols = pl.ds(pl.multiple_of(step * width, width), width)
        part = sqrt_tau * jnp.dot(picked_ref[...], chol_ref[:, cols], preferred_element_type=jnp.float32)
        for row in range(GROUP):
            spread(part[:, row * orbitals : (row + 1) * orbitals], acc_ref, row, count, w_local, GROUP)
        for lane in range(orbitals // LANES):
            out_ref[:, :, :, lane * LANES : (lane + 1) * LANES] = (
                acc_ref[lane].reshape(count, w_local, GROUP, LANES).astype(jnp.bfloat16)
            )

    out = pl.pallas_call(
        body,
        out_shape=jax.ShapeDtypeStruct((count, w_local, rows, orbitals), jnp.bfloat16),
        grid=(rows // GROUP,),
        in_specs=[VMEM, VMEM],
        out_specs=pl.BlockSpec((count, w_local, GROUP, orbitals), lambda i: (0, 0, i, 0)),
        scratch_shapes=[
            pltpu.VMEM((count * height, LANES), jnp.float32),
            pltpu.VMEM((walkers, vectors), jnp.bfloat16),
            pltpu.VMEM((walkers, vectors), jnp.bfloat16),
            pltpu.VMEM((orbitals // LANES, walkers * GROUP, LANES), jnp.float32),
        ],
        compiler_params=params(12),
        name="potential",
    )(blocks, chol)
    return out.reshape(count, w_local * rows, orbitals)


def choose_parents(inner, own, outer, src_shift, src_slot):
    def body(inner_ref, own_ref, outer_ref, from_ref, slot_ref, out_ref):
        side = 1 - 2 * lax.rem(lax.axis_index("pair"), 2)
        for walker in range(own.shape[0]):
            for offset, side_ref in ((-1, outer_ref), (0, own_ref), (1, inner_ref)):

                @pl.when(from_ref[walker] * side == offset)
                def _():
                    out_ref[walker] = side_ref[slot_ref[walker]]

    return pl.pallas_call(
        body,
        out_shape=jax.ShapeDtypeStruct(own.shape, jnp.bfloat16),
        in_specs=[VMEM, VMEM, VMEM, SMEM, SMEM],
        out_specs=VMEM,
        compiler_params=params(4),
        name="choose_parents",
    )(inner, own, outer, src_shift, src_slot)


def propagate(blocks, one_body, parents):
    w_local, orbitals, _ = parents.shape
    count = blocks.shape[0]
    rows = orbitals // count

    def body(blocks_ref, one_ref, parents_ref, out_ref, mat_ref):
        one = one_ref[...].astype(jnp.float32).reshape(count, rows, orbitals)
        for walker in range(w_local):
            mine = blocks_ref[:, walker * rows : (walker + 1) * rows, :].astype(jnp.float32)
            mat_ref[walker] = (mine + one).reshape(orbitals, orbitals).astype(jnp.bfloat16)
        terms = [parents_ref[walker] for walker in range(w_local)]
        totals = [term.astype(jnp.float32) for term in terms]
        for order in range(1, TERMS):
            products = [
                jnp.dot(mat_ref[walker], terms[walker], preferred_element_type=jnp.float32) * (1.0 / order)
                for walker in range(w_local)
            ]
            totals = [total + product for total, product in zip(totals, products)]
            terms = [product.astype(jnp.bfloat16) for product in products]
        for walker in range(w_local):
            out_ref[walker] = totals[walker].astype(jnp.bfloat16)

    return pl.pallas_call(
        body,
        out_shape=jax.ShapeDtypeStruct(parents.shape, jnp.bfloat16),
        in_specs=[VMEM, VMEM, VMEM],
        out_specs=VMEM,
        scratch_shapes=[pltpu.VMEM((w_local, orbitals, orbitals), jnp.bfloat16)],
        compiler_params=params(16),
        name="propagate",
    )(blocks, one_body, parents)


def plain(chol, walkers, trial, one_body, fields, src_shift, src_slot):
    count = lax.axis_size("pair")
    w_local, orbitals, _ = walkers.shape
    moved = lax.all_to_all(walkers, "pair", split_axis=1, concat_axis=0, tiled=True)
    formed = jnp.einsum("wia,ka->wik", moved, trial, preferred_element_type=jnp.float32)
    green_rows = formed.astype(jnp.bfloat16).reshape(moved.shape[0], moved.shape[1] * orbitals)
    partial_bias = lax.dot_general(
        green_rows, chol, (((1,), (1,)), ((), ())), preferred_element_type=jnp.float32
    )
    partials = exchange(partial_bias).reshape(count, w_local, -1)
    total = jnp.sum(partials, axis=0)
    shift = (fields - jnp.clip(sqrt_tau * total, -bias_cap, bias_cap)).astype(jnp.bfloat16)
    shifts = exchange(jnp.broadcast_to(shift[None], (count,) + shift.shape))
    shifts = shifts.reshape(count * w_local, -1)
    local_potential = (sqrt_tau * jnp.dot(shifts, chol, preferred_element_type=jnp.float32)).astype(
        jnp.bfloat16
    )
    own_potential = lax.all_to_all(local_potential, "pair", split_axis=0, concat_axis=1, tiled=True)
    amat = own_potential.astype(jnp.float32).reshape(w_local, orbitals, orbitals) + one_body.astype(
        jnp.float32
    )
    amat = amat.astype(jnp.bfloat16)
    term = walkers
    total = walkers.astype(jnp.float32)
    for order in range(1, TERMS):
        product = jnp.einsum("wik,wka->wia", amat, term, preferred_element_type=jnp.float32) / order
        total = total + product
        term = product.astype(jnp.bfloat16)
    propagated = total.astype(jnp.bfloat16)
    low, high = neighbours(propagated)
    position = (src_shift + 1) * w_local + src_slot
    return jnp.take(jnp.concatenate([low, propagated, high], axis=0), position, axis=0)


def held(chol, walkers, trial, one_body, fields, src_shift, src_slot):
    count = lax.axis_size("pair")
    w_local, orbitals, _ = walkers.shape

    inner_pairs, outer_pairs = partners(count)
    outer = lax.ppermute(walkers, "pair", outer_pairs)
    inner = lax.ppermute(walkers, "pair", inner_pairs)
    sent = pack(walkers, count)
    moved = exchange(sent)
    partial = bias_partial(moved, trial, chol, w_local)
    partials = exchange(partial)
    blocks = exchange(shift_blocks(partials, fields, src_shift, src_slot))
    sent = potential(blocks, chol, w_local, orbitals)
    received = exchange(sent)
    chosen = choose_parents(inner, walkers, outer, src_shift, src_slot)
    return propagate(received, one_body, chosen)


def shards(chol, walkers, *rest):
    rows = chol.shape[1] // walkers.shape[1]
    fits = 2 * chol.size <= 32 * MIB and rows % 16 == 0 and chol.shape[0] % LANES == 0
    walkers_all = walkers.shape[0] * lax.axis_size("pair")
    fits = fits and lax.axis_size("pair") % 2 == 0 and walkers_all % 16 == 0 and walkers_all < TILE
    fits = fits and chol.shape[1] % (UNITS * TILE) == 0 and chol.shape[0] % TILE == 0
    fits = fits and walkers.shape[1] == UNITS * TILE and walkers.shape[2] < TILE
    fits = fits and rows * walkers_all <= HELD_ROWS
    fits = fits and TILE < chol.shape[0] and chol.shape[0] - TILE + walkers_all <= HELD_ROWS
    return (held if fits else plain)(chol, walkers, *rest)


def solution(mesh):
    placed = (
        P("groups", "pair"),
        P(("groups", "pair"), None, None),
        P("groups", None),
        P("groups", None),
        P(("groups", "pair"), None),
        P(("groups", "pair")),
        P(("groups", "pair")),
    )
    return jax.shard_map(
        shards,
        mesh=mesh,
        in_specs=placed,
        out_specs=P(("groups", "pair"), None, None),
        check_vma=False,
    )
```
